128 devices in a mesh: lon: 32 (over x, z, core), lat: 4 (over y).
Axes of the slice: x: 4, y: 4, z: 4, core: 2. Of those that a mesh axis runs over, the one named last changes fastest.
Arguments:
- obs_values: bfloat16 [16384, 31, 256], P(('lon', 'lat')), may hold values from -6 to 6
- obs_offset: float32 [16384, 2, 256], P(('lon', 'lat')), may hold values from -0.5 to 0.5
- obs_cell: int32 [16384, 256], P(('lon', 'lat')), may hold values from 0 to 511
- obs_slot: int32 [16384, 256], P(('lon', 'lat')), may hold values from 0 to 11
- obs_count: int32 [128, 128], P(('lon', 'lat')), may hold values from 1 to 256, as said below
- embed_weight: bfloat16 [384, 256], replicated, may hold values from -0.3125 to 0.3125
- embed_bias: float32 [256], replicated, may hold values from -3 to 3
- stride_weight: bfloat16 [9, 256, 256], replicated, may hold values from -0.125 to 0.125
- stride_bias: float32 [256], replicated, may hold values from -3 to 3
- depth_weight: float32 [9, 256], replicated, may hold values from -2 to 2
- norm_gain: float32 [256], replicated, may hold values from 0.1 to 1.9
Outputs:
- encoded: bfloat16 [32, 512, 256], P('lat', 'lon')
The draws below stay inside these ranges and needn't reach their ends.
Inputs may be any that keep to these rules, and one draw needn't show every extreme that they name: `obs_count`: every entry is at least 1; in every draw one destination tile receives exactly 256 live slots from every source shard.
All inputs are finite; a program needn't handle non-finite values.
Results may differ from the reference program's by a relative error of at most 0.011.
Values may be sent and summed in bfloat16 or wider, within the bound.
A program may use at most 128 MiB of HBM per device.

```python
import jax
import jax.numpy as jnp
from jax import lax

D = 256
OBS_VARS = 31
SLOTS = 12
TLAT = 16
TLON = 32
CAP = 256
LAT_TILES = 4
NTILES = 128
CELLS = 512
GLAT = 64
GLON = 1024


def draw_obs_count(key, part):
    base_key = jax.random.fold_in(key, 11)
    heat_key, level_key, hot_key = jax.random.split(base_key, 3)
    heat = jax.random.randint(heat_key, (NTILES,), 1, 5, dtype=jnp.int32)
    level = jax.random.randint(level_key, (NTILES, NTILES), 0, CAP + 1, dtype=jnp.int32)
    counts = jnp.maximum(1, level * heat[None, :] // 4)
    hottest = jax.random.randint(hot_key, (), 0, NTILES, dtype=jnp.int32)
    column = jnp.arange(NTILES, dtype=jnp.int32)[None, :]
    counts = jnp.where(column == hottest, CAP, counts)
    return counts.astype(jnp.int32)


def plant(values, stream_key, smallest, top_value):
    longest = values.shape.index(max(values.shape))
    spots = []
    for shift in (0, 1):
        where = [jax.random.randint(jax.random.fold_in(stream_key, axis), (), 0, length) for axis, length in enumerate(values.shape)]
        where[longest] = (where[longest] + shift) % values.shape[longest]
        spots.append(tuple(where))
    return values.at[spots[0]].set(smallest).at[spots[1]].set(top_value)


def block_scale(key, shape, pieces, smallest, high):
    def one(axis_at, blocks):
        draws = jax.random.uniform(jax.random.fold_in(jax.random.fold_in(key, 6), axis_at), (blocks,), jnp.float32, smallest / len(pieces), high / len(pieces))
        return jnp.repeat(jnp.exp(draws), shape[axis_at] // blocks).reshape((-1,) + (1,) * (len(shape) - axis_at - 1))

    factor_of = one(*pieces[0])
    for cut in pieces[1:]:
        factor_of = factor_of * one(*cut)
    return factor_of


def noise(own_key, extent, scale, most, cuts=(), held_as=jnp.bfloat16):
    gain = block_scale(own_key, extent, cuts, -0.22, 0.18) if cuts else 1.0
    array = jax.random.normal(own_key, extent, jnp.float32) * scale * gain
    return jnp.minimum(jnp.maximum(array, -most), most).astype(held_as)


def setup_inputs(seed: int = 0) -> dict:
    key_list = jax.random.split(jax.random.key(seed), 12)
    return {
        "obs_values": noise(key_list[0], (NTILES * NTILES, OBS_VARS, CAP), 1.0, 6.0, ((0, 128),)),
        "obs_offset": jnp.clip(jax.random.uniform(key_list[1], (NTILES * NTILES, 2, CAP), jnp.float32, -0.5, 0.5) * block_scale(key_list[1], (NTILES * NTILES, 2, CAP), ((0, 128),), -0.4, 0.0), -0.5, 0.5),
        "obs_cell": plant(jax.random.randint(key_list[2], (NTILES * NTILES, CAP), 0, CELLS), jax.random.fold_in(key_list[2], 1), 0, CELLS - 1).astype(jnp.int32),
        "obs_slot": plant(jax.random.randint(key_list[3], (NTILES * NTILES, CAP), 0, SLOTS), jax.random.fold_in(key_list[3], 1), 0, SLOTS - 1).astype(jnp.int32),
        "obs_count": draw_obs_count(jax.random.fold_in(key_list[11], 71), 0),
        "embed_weight": noise(key_list[5], (SLOTS * (OBS_VARS + 1), D), (SLOTS * (OBS_VARS + 1)) ** -0.5, 0.3125),
        "embed_bias": noise(key_list[6], (D,), 0.5, 3.0, (), jnp.float32),
        "stride_weight": noise(key_list[7], (9, D, D), (9 * D) ** -0.5, 0.125),
        "stride_bias": noise(key_list[8], (D,), 0.5, 3.0, (), jnp.float32),
        "depth_weight": noise(key_list[9], (9, D), 9 ** -0.5, 2.0, (), jnp.float32),
        "norm_gain": jnp.clip(1.0 + 0.18 * jax.random.normal(key_list[10], (D,), jnp.float32), 0.1, 1.9),
    }


def layer_norm(mixed, norm_gain):
    centre = mixed - lax.optimization_barrier(jnp.mean(mixed, axis=-1, keepdims=True))
    spread = lax.optimization_barrier(jnp.mean(centre * centre, axis=-1, keepdims=True))
    return centre * lax.rsqrt(spread + 1e-05) * norm_gain

def reference(obs_values, obs_offset, obs_cell, obs_slot, obs_count, embed_weight, embed_bias, stride_weight, stride_bias, depth_weight, norm_gain):
    tiles = NTILES
    width = OBS_VARS + 1
    position = lax.broadcasted_iota(jnp.int32, obs_cell.shape, 1)
    live = position < obs_count.reshape(-1)[:, None]
    radius = obs_offset[:, 0, :] * obs_offset[:, 0, :] + obs_offset[:, 1, :] * obs_offset[:, 1, :]
    weight = jnp.where(live, jnp.exp(-2.0 * radius), jnp.float32(0.0))
    scaled = obs_values.astype(jnp.float32) * weight[:, None, :]
    packed = jnp.concatenate([scaled, weight[:, None, :]], axis=1).astype(jnp.bfloat16)
    target = jnp.arange(tiles * tiles, dtype=jnp.int32) % tiles
    lon_tile = (target // LAT_TILES).astype(jnp.int32)
    lat_tile = (target % LAT_TILES).astype(jnp.int32)
    grid_row = lat_tile[:, None] * TLAT + obs_cell // TLON
    grid_col = lon_tile[:, None] * TLON + obs_cell % TLON
    segment = ((obs_slot * GLAT + grid_row) * GLON + grid_col).astype(jnp.int32)
    data = jnp.transpose(packed, (0, 2, 1)).reshape(-1, width).astype(jnp.float32)
    total = jax.ops.segment_sum(data, segment.reshape(-1), num_segments=SLOTS * GLAT * GLON)
    total = jnp.transpose(total.reshape(SLOTS, GLAT, GLON, width), (1, 2, 0, 3))
    density = total[..., width - 1:]
    ratio = total[..., :width - 1] / (1.0 + density)
    gridded = jnp.concatenate([ratio, density], axis=3).reshape(GLAT * GLON, SLOTS * width).astype(jnp.bfloat16)
    projected = jnp.dot(gridded, embed_weight, preferred_element_type=jnp.float32) + embed_bias
    embedded = jax.nn.gelu(projected).astype(jnp.bfloat16).reshape(GLAT, GLON, D)
    framed = jnp.concatenate([jnp.zeros((1, GLON, D), jnp.bfloat16), embedded], axis=0)
    framed = jnp.concatenate([framed[:, GLON - 1:], framed], axis=1)
    patches = jnp.concatenate([framed[row_at:row_at + GLAT - 1:2, col_at:col_at + GLON - 1:2] for row_at in range(3) for col_at in range(3)], axis=2)
    strided = jnp.dot(patches.reshape(-1, 9 * D), stride_weight.reshape(9 * D, D), preferred_element_type=jnp.float32) + stride_bias
    coarse = jax.nn.gelu(strided).astype(jnp.bfloat16).reshape(GLAT // 2, GLON // 2, D)
    wide = jnp.concatenate([coarse[:, -1:], coarse, coarse[:, :1]], axis=1)
    zero_row = jnp.zeros((1, GLON // 2 + 2, D), jnp.bfloat16)
    full = jnp.concatenate([zero_row, wide, zero_row], axis=0).astype(jnp.float32)
    depth = jnp.zeros((GLAT // 2, GLON // 2, D), jnp.float32)
    for row_at in range(3):
        for col_at in range(3):
            depth = depth + full[row_at:row_at + GLAT // 2, col_at:col_at + GLON // 2] * depth_weight[3 * row_at + col_at]
    mixed = coarse.astype(jnp.float32) + depth
    return layer_norm(mixed, norm_gain).astype(jnp.bfloat16)
```

```python
import functools

import jax
import jax.numpy as jnp
import numpy as np
from jax import lax
from jax.experimental import pallas as pl
from jax.experimental.pallas import tpu as pltpu
from jax.sharding import PartitionSpec as P

MESH = pl.DeviceIdType.MESH
D = 256
OBS_VARS = 31
WIDTH = 32
SLOTS = 12
TLAT = 16
TLON = 32
CELLS = 512
GROUP = 8
BF16 = jnp.bfloat16
F32 = jnp.float32


def cell_number(row, col):
    return ((row % 2) * 2 + col % 2) * 128 + (row // 2) * 16 + col // 2


def strip_table():
    table = np.zeros((80, CELLS), np.float32)
    for row in range(TLAT):
        for i in range(3):
            table[row * 3 + i, cell_number(row, TLON - 3 + i)] = 1
        for i in range(2):
            table[48 + row * 2 + i, cell_number(row, i)] = 1
    return table


def rim_table():
    table = np.zeros((4, 12, 16, 256), np.float32)
    for plane in range(4):
        row_odd, col_odd = divmod(plane, 2)
        for p in range(-2, 9):
            row = 2 * p + row_odd
            if row < -3 or row > 17:
                continue
            for q in (-2, -1, 16):
                if q == -2 and not col_odd:
                    continue
                if q < 0:
                    i = 2 * q + col_odd + 3
                    if row < 0:
                        source = 80 + (row + 16) * 3 + i - 32
                    elif row < 16:
                        source = row * 3 + i
                    else:
                        source = 112 + (row - 16) * 3 + i
                    table[plane, p + 2, 16 + q, source] = 1
                else:
                    i = col_odd
                    if row < 0:
                        source = 96 + (row + 16) * 2 + i - 16
                    elif row < 16:
                        source = 48 + row * 2 + i
                    else:
                        source = 128 + (row - 16) * 2 + i
                    table[plane, p + 3, 0, source] = 1
    return table.reshape(4 * 12 * 16, 256)


def gelu(x):
    return 0.5 * x * (1.0 + jnp.tanh(0.7978845608028654 * (x + 0.044715 * (x * x * x))))


def far_first(dims):
    nx, nz, nc, ny = dims
    offsets = [
        (dx, dz, dc, dy)
        for dx in range(nx)
        for dz in range(nz)
        for dc in range(nc)
        for dy in range(ny)
        if dx or dz or dc or dy
    ]
    scrambled = sorted(offsets, key=lambda o: (o[0] * 37 + o[1] * 59 + o[2] * 83 + o[3] * 101) % 127)

    def length(o):
        return min(o[0], nx - o[0]) + min(o[1], nz - o[1]) + min(o[3], ny - o[3])

    return sorted(scrambled, key=lambda o: -length(o))


def kernel(
    dims,
    values_ref,
    offset_ref,
    cell_ref,
    slot_ref,
    count_ref,
    embed_weight_hbm,
    embed_bias_ref,
    stride_weight_hbm,
    stride_bias_ref,
    depth_weight_ref,
    gain_ref,
    strip_hbm,
    rim_hbm,
    out_ref,
    aux_ref,
    recv_ref,
    recv_aux_ref,
    spread_ref,
    hot_ref,
    total_ref,
    embed_weight_ref,
    stride_weight_ref,
    strip_ref,
    rim_ref,
    tile_ref,
    strips_ref,
    halo_ref,
    framed_ref,
    send_sem,
    recv_sem,
    local_sem,
    halo_send_sem,
    halo_recv_sem,
):
    nx, nz, nc, ny = dims
    lons = nx * nz * nc
    tiles = lons * ny
    groups = tiles // GROUP
    lon, lat = lax.axis_index("lon"), lax.axis_index("lat")
    core = lon % nc
    z = (lon // nc) % nz
    x = lon // (nc * nz)

    def wrapped(value, size):
        return jnp.where(value >= size, value - size, value)

    at_x = [wrapped(x + i, nx) * (nz * nc) for i in range(nx)]
    at_z = [wrapped(z + i, nz) * nc for i in range(nz)]
    at_core = [wrapped(core + i, nc) for i in range(nc)]
    at_y = [wrapped(lat + i, ny) for i in range(ny)]
    order = far_first(dims)
    partners = [(at_x[o[0]] + at_z[o[1]] + at_core[o[2]], at_y[o[3]]) for o in order]

    barrier = pltpu.get_barrier_semaphore()
    for partner in partners:
        pl.semaphore_signal(barrier, inc=1, device_id=partner, device_id_type=MESH)

    halo_ref[...] = jnp.zeros_like(halo_ref)
    me = lon * ny + lat
    own = pltpu.make_async_copy(values_ref.at[me], recv_ref.at[0], local_sem.at[0])
    own.start()
    loads = [
        pltpu.make_async_copy(source, target, local_sem.at[i])
        for i, (source, target) in enumerate(
            (
                (embed_weight_hbm, embed_weight_ref),
                (stride_weight_hbm, stride_weight_ref),
                (strip_hbm, strip_ref),
                (rim_hbm, rim_ref),
            ),
            1,
        )
    ]

    lane = lax.broadcasted_iota(jnp.int32, (tiles, tiles), 1)
    line = lax.broadcasted_iota(jnp.int32, (tiles, tiles), 0)
    count = jnp.sum(
        jnp.where(lane == line, count_ref[...].astype(F32), 0.0), axis=1, keepdims=True
    )
    position = lax.broadcasted_iota(jnp.int32, cell_ref.shape, 1).astype(F32)
    off_y, off_x = offset_ref[:, 0, :], offset_ref[:, 1, :]
    weight = jnp.where(position < count, jnp.exp(-2.0 * (off_y * off_y + off_x * off_x)), 0.0)
    cell = cell_ref[...]
    row, col = cell >> 5, cell & 31
    code = (
        slot_ref[...] * CELLS
        + (((row & 1) * 2 + (col & 1)) * 128 + (row >> 1) * 16 + (col >> 1))
    ).astype(F32)
    aux_ref[:, 0, :] = weight
    aux_ref[:, 1, :] = code

    pl.semaphore_wait(barrier, tiles - 1)

    def send_values(source, target, sem, partner):
        return pltpu.make_async_remote_copy(
            values_ref.at[source],
            recv_ref.at[target],
            send_sem.at[0],
            recv_sem.at[sem],
            device_id=partner,
            device_id_type=MESH,
        )

    def send_aux(source, target, sem, partner):
        return pltpu.make_async_remote_copy(
            aux_ref.at[source],
            recv_aux_ref.at[target],
            send_sem.at[1],
            recv_sem.at[sem + groups],
            device_id=partner,
            device_id_type=MESH,
        )

    for i, partner in enumerate(partners, 1):
        to = partner[0] * ny + partner[1]
        send_aux(to, i, i // GROUP, partner).start()
        send_values(to, i, i // GROUP, partner).start()

    for load in loads:
        load.start()
    own_aux = pltpu.make_async_copy(aux_ref.at[me], recv_aux_ref.at[0], local_sem.at[5])
    own_aux.start()
    total_ref[...] = jnp.zeros_like(total_ref)
    own.wait()
    own_aux.wait()

    cells = lax.broadcasted_iota(jnp.int32, (CELLS, 256), 0).astype(F32)

    def scatter(group):
        def build(i, carry):
            at = group * GROUP + i
            w = recv_aux_ref[at, 0:1, :]
            code = recv_aux_ref[at, 1:2, :]
            slot = jnp.floor(code * (1.0 / CELLS))
            cell = code - slot * CELLS
            scaled = recv_ref[at].astype(F32) * w
            packed = jnp.concatenate([scaled, w], axis=0)
            lanes = pl.ds(pl.multiple_of(i * 256, 256), 256)
            for s in range(SLOTS):
                spread_ref[s * WIDTH : (s + 1) * WIDTH, lanes] = jnp.where(
                    slot == s, packed, 0.0
                ).astype(BF16)
            hot_ref[:, lanes] = jnp.where(cells == cell, 1.0, 0.0).astype(BF16)
            return carry

        lax.fori_loop(0, GROUP, build, 0)
        total_ref[...] += lax.dot_general(
            spread_ref[...],
            hot_ref[...],
            (((1,), (1,)), ((), ())),
            preferred_element_type=F32,
        )

    def arrive(group, first, size):
        send_aux(pl.ds(first, size), pl.ds(first, size), group, partners[0]).wait_recv()
        send_values(pl.ds(first, size), pl.ds(first, size), group, partners[0]).wait_recv()

    def group_step(group, carry):
        @pl.when(group == 0)
        def _():
            arrive(0, 1, GROUP - 1)

        @pl.when(group > 0)
        def _():
            arrive(group, group * GROUP, GROUP)

        scatter(group)
        return carry

    lax.fori_loop(0, groups, group_step, 0)

    for load in loads:
        load.wait()

    total = total_ref[...].reshape(SLOTS, WIDTH, CELLS)
    density = total[:, WIDTH - 1 :, :]
    variable = lax.broadcasted_iota(jnp.int32, (SLOTS, WIDTH, CELLS), 1)
    gridded = jnp.where(variable == WIDTH - 1, total, total / (1.0 + density))
    gridded = gridded.reshape(SLOTS * WIDTH, CELLS).astype(BF16)
    projected = lax.dot_general(
        gridded, embed_weight_ref[...], (((0,), (0,)), ((), ())), preferred_element_type=F32
    )
    embedded = gelu(projected + embed_bias_ref[...]).astype(BF16)
    tile_ref[...] = embedded.reshape(4, 8, 16, D)
    strips_ref[...] = jnp.dot(strip_ref[...], embedded, preferred_element_type=F32).astype(BF16)

    right, left = wrapped(lon + 1, lons), wrapped(lon + lons - 1, lons)
    below, above = wrapped(lat + 1, ny), wrapped(lat + ny - 1, ny)

    def rows(i, source, target, partner):
        return pltpu.make_async_remote_copy(
            source,
            target,
            halo_send_sem.at[i],
            halo_recv_sem.at[i],
            device_id=partner,
            device_id_type=MESH,
        )

    exchange = [
        rows(0, tile_ref.at[2:4, 6:8], framed_ref.at[2:4, 0:2, 1], (lon, below)),
        rows(1, tile_ref.at[0:2, 7:8], framed_ref.at[0:2, 1:2, 1], (lon, below)),
        rows(2, tile_ref.at[0:4, 0:1], framed_ref.at[0:4, 10:11, 1], (lon, above)),
        rows(3, strips_ref.at[0:48], halo_ref.at[0:48], (right, lat)),
        rows(4, strips_ref.at[48:80], halo_ref.at[48:80], (left, lat)),
        rows(5, strips_ref.at[32:48], halo_ref.at[80:96], (right, below)),
        rows(6, strips_ref.at[64:80], halo_ref.at[96:112], (left, below)),
        rows(7, strips_ref.at[0:16], halo_ref.at[112:128], (right, above)),
        rows(8, strips_ref.at[48:64], halo_ref.at[128:144], (left, above)),
    ]
    for copy in reversed(exchange):
        copy.start()
    framed_ref[:, 2:10, 1] = embedded.reshape(4, 8, 16, D)
    for copy in exchange:
        copy.wait_recv()

    @pl.when(lat == 0)
    def _():
        halo_ref[80:112] = jnp.zeros((32, D), BF16)
        framed_ref[2:4, 1, 1] = jnp.zeros((2, 16, D), BF16)

    rim = jnp.dot(rim_ref[...], halo_ref[...], preferred_element_type=F32).astype(BF16)
    framed_ref[:, :, 0] = rim.reshape(4, 12, 16, D)

    planes = [framed_ref[i].reshape(384, D) for i in range(4)]
    span = 336

    def tap(a, c):
        plane = planes[(0 if a == 1 else 2) + (0 if c == 1 else 1)]
        base = 0 if a == 0 else 32
        return jnp.dot(
            plane[base : base + span], stride_weight_ref[3 * a + c], preferred_element_type=F32
        )

    before = tap(0, 0) + tap(1, 0) + tap(2, 0)
    here = tap(0, 1) + tap(1, 1) + tap(2, 1) + tap(0, 2) + tap(1, 2) + tap(2, 2)
    strided = pltpu.roll(before, 1, 0) + here + stride_bias_ref[...]
    coarse = gelu(strided).astype(BF16).astype(F32)
    at = lax.broadcasted_iota(jnp.int32, (span, D), 0)
    low = jnp.where(lat == 0, 40, 0)
    high = jnp.where(lat == ny - 1, 296, span)
    coarse = jnp.where((at >= low) & (at < high), coarse, 0.0)

    reach = 272

    def column(c):
        total = coarse[0:reach] * depth_weight_ref[c : c + 1]
        for a in (1, 2):
            total = total + coarse[32 * a : 32 * a + reach] * depth_weight_ref[3 * a + c : 3 * a + c + 1]
        return total

    mixed = (
        coarse[32 : 32 + reach]
        + column(1)
        + pltpu.roll(column(0), 1, 0)
        + pltpu.roll(column(2), reach - 1, 0)
    )
    mixed = mixed[:256].reshape(8, 2, 16, D)[:, 1]
    centre = mixed - jnp.mean(mixed, axis=-1, keepdims=True)
    variance = jnp.mean(centre * centre, axis=-1, keepdims=True)
    out_ref[...] = (centre * lax.rsqrt(variance + 1e-05) * gain_ref[...][None]).astype(BF16)

    for copy in exchange:
        copy.wait_send()
    send_aux(pl.ds(1, tiles - 1), pl.ds(1, tiles - 1), 0, partners[0]).wait_send()
    send_values(pl.ds(1, tiles - 1), pl.ds(1, tiles - 1), 0, partners[0]).wait_send()


def physical(lons, lats):
    nc = 2
    nz = 4 if lons % 8 == 0 else 2
    return (lons // (nc * nz), nz, nc, lats)


def solution(mesh):
    dims = physical(mesh.shape["lon"], mesh.shape["lat"])
    tiles = mesh.shape["lon"] * mesh.shape["lat"]
    groups = tiles // GROUP
    vmem = pl.BlockSpec(memory_space=pltpu.VMEM)
    anywhere = pl.BlockSpec(memory_space=pl.ANY)
    strips, rims = strip_table(), rim_table()

    def on_device(
        obs_values,
        obs_offset,
        obs_cell,
        obs_slot,
        obs_count,
        embed_weight,
        embed_bias,
        stride_weight,
        stride_bias,
        depth_weight,
        norm_gain,
    ):
        return pl.pallas_call(
            functools.partial(kernel, dims),
            out_shape=jax.ShapeDtypeStruct((TLAT // 2, TLON // 2, D), BF16),
            in_specs=[
                anywhere,
                vmem,
                vmem,
                vmem,
                vmem,
                anywhere,
                vmem,
                anywhere,
                vmem,
                vmem,
                vmem,
                anywhere,
                anywhere,
            ],
            out_specs=vmem,
            scratch_shapes=[
                pltpu.VMEM((tiles, 2, 256), F32),
                pltpu.VMEM((tiles, OBS_VARS, 256), BF16),
                pltpu.VMEM((tiles, 2, 256), F32),
                pltpu.VMEM((SLOTS * WIDTH, GROUP * 256), BF16),
                pltpu.VMEM((CELLS, GROUP * 256), BF16),
                pltpu.VMEM((SLOTS * WIDTH, CELLS), F32),
                pltpu.VMEM((SLOTS * WIDTH, D), BF16),
                pltpu.VMEM((9, D, D), BF16),
                pltpu.VMEM((80, CELLS), BF16),
                pltpu.VMEM((768, 256), BF16),
                pltpu.VMEM((4, 8, 16, D), BF16),
                pltpu.VMEM((80, D), BF16),
                pltpu.VMEM((256, D), BF16),
                pltpu.VMEM((4, 12, 2, 16, D), BF16),
                pltpu.SemaphoreType.DMA((2,)),
                pltpu.SemaphoreType.DMA((2 * groups,)),
                pltpu.SemaphoreType.DMA((6,)),
                pltpu.SemaphoreType.DMA((9,)),
                pltpu.SemaphoreType.DMA((9,)),
            ],
            compiler_params=pltpu.CompilerParams(
                collective_id=0, has_side_effects=True, vmem_limit_bytes=60 << 20
            ),
        )(
            obs_values,
            obs_offset,
            obs_cell,
            obs_slot,
            obs_count,
            embed_weight,
            embed_bias[None],
            stride_weight,
            stride_bias[None],
            depth_weight,
            norm_gain[None],
            jnp.asarray(strips, BF16),
            jnp.asarray(rims, BF16),
        )

    placed = (
        P(("lon", "lat"), None, None),
        P(("lon", "lat"), None, None),
        P(("lon", "lat"), None),
        P(("lon", "lat"), None),
        P(("lon", "lat"), None),
        P(),
        P(),
        P(),
        P(),
        P(),
        P(),
    )
    return jax.shard_map(
        on_device, mesh=mesh, in_specs=placed, out_specs=P("lat", "lon", None), check_vma=False
    )
```

```python
import functools

import jax
import jax.numpy as jnp
import numpy as np
from jax import lax
from jax.experimental import pallas as pl
from jax.experimental.pallas import tpu as pltpu
from jax.sharding import PartitionSpec as P

MESH = pl.DeviceIdType.MESH
D = 256
OBS_VARS = 31
WIDTH = 32
SLOTS = 12
TLAT = 16
TLON = 32
CELLS = 512
GROUP = 8
BF16 = jnp.bfloat16
F32 = jnp.float32
PITCH = 136


def cell_number(row, col):
    return ((row % 2) * 2 + col % 2) * 128 + (row // 2) * 16 + col // 2


def strip_table():
    table = np.zeros((80, CELLS), np.float32)
    for row in range(TLAT):
        for i in range(3):
            table[row * 3 + i, cell_number(row, TLON - 3 + i)] = 1
        for i in range(2):
            table[48 + row * 2 + i, cell_number(row, i)] = 1
    return table


def rim_table():
    table = np.zeros((4, 12, 16, 256), np.float32)
    for plane in range(4):
        row_odd, col_odd = divmod(plane, 2)
        for p in range(-2, 9):
            row = 2 * p + row_odd
            if row < -3 or row > 17:
                continue
            for q in (-2, -1, 16):
                if q == -2 and not col_odd:
                    continue
                if q < 0:
                    i = 2 * q + col_odd + 3
                    if row < 0:
                        source = 80 + (row + 16) * 3 + i - 32
                    elif row < 16:
                        source = row * 3 + i
                    else:
                        source = 112 + (row - 16) * 3 + i
                    table[plane, p + 2, 16 + q, source] = 1
                else:
                    i = col_odd
                    if row < 0:
                        source = 96 + (row + 16) * 2 + i - 16
                    elif row < 16:
                        source = 48 + row * 2 + i
                    else:
                        source = 128 + (row - 16) * 2 + i
                    table[plane, p + 3, 0, source] = 1
    return table.reshape(4 * 12 * 16, 256)


def gelu(x):
    return 0.5 * x * (1.0 + jnp.tanh(0.7978845608028654 * (x + 0.044715 * (x * x * x))))


def far_first(dims):
    nx, nz, nc, ny = dims
    offsets = [
        (dx, dz, dc, dy)
        for dx in range(nx)
        for dz in range(nz)
        for dc in range(nc)
        for dy in range(ny)
        if dx or dz or dc or dy
    ]
    scrambled = sorted(offsets, key=lambda o: (o[0] * 37 + o[1] * 59 + o[2] * 83 + o[3] * 101) % 127)

    def length(o):
        return min(o[0], nx - o[0]) + min(o[1], nz - o[1]) + min(o[3], ny - o[3])

    return sorted(scrambled, key=lambda o: -length(o))


def kernel(
    dims,
    values_ref,
    offset_ref,
    cell_ref,
    slot_ref,
    count_ref,
    embed_weight_hbm,
    embed_bias_ref,
    stride_weight_hbm,
    stride_bias_ref,
    depth_weight_ref,
    gain_ref,
    strip_hbm,
    rim_hbm,
    out_ref,
    raw_ref,
    wide_ref,
    packed_ref,
    code_ref,
    recv_ref,
    recv_code_ref,
    spread_ref,
    hot_ref,
    total_ref,
    embed_weight_ref,
    stride_weight_ref,
    strip_ref,
    rim_ref,
    tile_ref,
    strips_ref,
    halo_ref,
    framed_ref,
    send_sem,
    recv_sem,
    local_sem,
    halo_send_sem,
    halo_recv_sem,
):
    nx, nz, nc, ny = dims
    lons = nx * nz * nc
    tiles = lons * ny
    groups = tiles // GROUP
    lon, lat = lax.axis_index("lon"), lax.axis_index("lat")
    core = lon % nc
    z = (lon // nc) % nz
    x = lon // (nc * nz)

    def wrapped(value, size):
        return jnp.where(value >= size, value - size, value)

    at_x = [wrapped(x + i, nx) * (nz * nc) for i in range(nx)]
    at_z = [wrapped(z + i, nz) * nc for i in range(nz)]
    at_core = [wrapped(core + i, nc) for i in range(nc)]
    at_y = [wrapped(lat + i, ny) for i in range(ny)]
    order = far_first(dims)
    partners = [(at_x[o[0]] + at_z[o[1]] + at_core[o[2]], at_y[o[3]]) for o in order]

    chunks = ((0, 8), (8, 16), (16, 24), (24, 31))
    raws = [
        pltpu.make_async_copy(
            values_ref.at[low:high], raw_ref.at[low:high], local_sem.at[5 + i]
        )
        for i, (low, high) in enumerate(chunks)
    ]
    for raw in raws:
        raw.start()
    barrier = pltpu.get_barrier_semaphore()
    for partner in partners:
        pl.semaphore_signal(barrier, inc=1, device_id=partner, device_id_type=MESH)

    halo_ref[...] = jnp.zeros_like(halo_ref)
    me = lon * ny + lat
    loads = [
        pltpu.make_async_copy(source, target, local_sem.at[i])
        for i, (source, target) in enumerate(
            (
                (embed_weight_hbm, embed_weight_ref),
                (stride_weight_hbm, stride_weight_ref),
                (strip_hbm, strip_ref),
                (rim_hbm, rim_ref),
            ),
            1,
        )
    ]

    lane = lax.broadcasted_iota(jnp.int32, (tiles, tiles), 1)
    line = lax.broadcasted_iota(jnp.int32, (tiles, tiles), 0)
    count = jnp.sum(
        jnp.where(lane == line, count_ref[...].astype(F32), 0.0), axis=1, keepdims=True
    )
    position = lax.broadcasted_iota(jnp.int32, cell_ref.shape, 1).astype(F32)
    off_y, off_x = offset_ref[:, 0, :], offset_ref[:, 1, :]
    weight = jnp.where(position < count, jnp.exp(-2.0 * (off_y * off_y + off_x * off_x)), 0.0)
    cell = cell_ref[...]
    row, col = cell >> 5, cell & 31
    code = (
        slot_ref[...] * CELLS
        + (((row & 1) * 2 + (col & 1)) * 128 + (row >> 1) * 16 + (col >> 1))
    ).astype(F32)
    code_ref[:, 0, :] = code
    def widen(k, row):
        for h in range(2):
            start = (h * WIDTH + k) * PITCH
            wide_ref[start : start + tiles] = row[:, h * 128 : h * 128 + 128]

    widen(31, weight)
    for raw, (low, high) in zip(raws, chunks):
        raw.wait()
        for k in range(low, high):
            widen(k, raw_ref[k].astype(F32) * weight)

    def pack(target):
        halves = [
            wide_ref[pl.ds(target + h * WIDTH * PITCH, WIDTH, stride=PITCH), :] for h in range(2)
        ]
        return jnp.concatenate(halves, axis=1).astype(BF16)

    pl.semaphore_wait(barrier, tiles - 1)

    def send_values(source, target, sem, partner):
        return pltpu.make_async_remote_copy(
            packed_ref.at[source],
            recv_ref.at[target],
            send_sem.at[0],
            recv_sem.at[sem],
            device_id=partner,
            device_id_type=MESH,
        )

    def send_code(source, target, sem, partner):
        return pltpu.make_async_remote_copy(
            code_ref.at[source],
            recv_code_ref.at[target],
            send_sem.at[1],
            recv_sem.at[sem + groups],
            device_id=partner,
            device_id_type=MESH,
        )

    for i, partner in enumerate(partners, 1):
        to = partner[0] * ny + partner[1]
        packed_ref[i] = pack(to)
        send_code(to, i, i // GROUP, partner).start()
        send_values(i, i, i // GROUP, partner).start()

    for load in loads:
        load.start()
    recv_ref[0] = pack(me)
    recv_code_ref[0] = code_ref[me]
    total_ref[...] = jnp.zeros_like(total_ref)

    line16 = lax.broadcasted_iota(jnp.int32, (16, 256), 0).astype(F32).astype(BF16)

    def scatter(group):
        def build(i, carry):
            at = group * GROUP + i
            code = recv_code_ref[at]
            slot = jnp.floor(code * (1.0 / CELLS))
            cell = code - slot * CELLS
            half = jnp.where(cell >= 256, 1.0, 0.0)
            low = cell - 256.0 * half
            first = jnp.broadcast_to(jnp.where(half == 0.0, low, -1.0), (16, 256)).astype(BF16)
            second = jnp.broadcast_to(jnp.where(half == 1.0, low, -1.0), (16, 256)).astype(BF16)
            slot = jnp.broadcast_to(slot, (16, 256)).astype(BF16)
            packed = recv_ref[at]
            lanes = pl.ds(pl.multiple_of(i * 256, 256), 256)
            zero, one = jnp.zeros((16, 256), BF16), jnp.ones((16, 256), BF16)
            for s in range(SLOTS):
                mine = slot == s
                for h in range(2):
                    spread_ref[s * WIDTH + h * 16 : s * WIDTH + h * 16 + 16, lanes] = jnp.where(
                        mine, packed[h * 16 : h * 16 + 16], zero
                    )
            for h, wanted in enumerate((first, second)):
                for r in range(16):
                    at_row = h * 256 + r * 16
                    hot_ref[at_row : at_row + 16, lanes] = jnp.where(
                        wanted == line16 + (r * 16), one, zero
                    )
            return carry

        lax.fori_loop(0, GROUP, build, 0, unroll=True)
        total_ref[...] += lax.dot_general(
            spread_ref[...],
            hot_ref[...],
            (((1,), (1,)), ((), ())),
            preferred_element_type=F32,
        )

    def arrive(group, first, size):
        send_code(pl.ds(first, size), pl.ds(first, size), group, partners[0]).wait_recv()
        send_values(pl.ds(first, size), pl.ds(first, size), group, partners[0]).wait_recv()

    def group_step(group, carry):
        @pl.when(group == 0)
        def _():
            arrive(0, 1, GROUP - 1)

        @pl.when(group > 0)
        def _():
            arrive(group, group * GROUP, GROUP)

        scatter(group)
        return carry

    lax.fori_loop(0, groups, group_step, 0)

    for load in loads:
        load.wait()

    total = total_ref[...].reshape(SLOTS, WIDTH, CELLS)
    density = total[:, WIDTH - 1 :, :]
    variable = lax.broadcasted_iota(jnp.int32, (SLOTS, WIDTH, CELLS), 1)
    gridded = jnp.where(variable == WIDTH - 1, total, total / (1.0 + density))
    gridded = gridded.reshape(SLOTS * WIDTH, CELLS).astype(BF16)
    projected = lax.dot_general(
        gridded, embed_weight_ref[...], (((0,), (0,)), ((), ())), preferred_element_type=F32
    )
    embedded = gelu(projected + embed_bias_ref[...]).astype(BF16)
    tile_ref[...] = embedded.reshape(4, 8, 16, D)
    strips_ref[...] = jnp.dot(strip_ref[...], embedded, preferred_element_type=F32).astype(BF16)

    right, left = wrapped(lon + 1, lons), wrapped(lon + lons - 1, lons)
    below, above = wrapped(lat + 1, ny), wrapped(lat + ny - 1, ny)

    def rows(i, source, target, partner):
        return pltpu.make_async_remote_copy(
            source,
            target,
            halo_send_sem.at[i],
            halo_recv_sem.at[i],
            device_id=partner,
            device_id_type=MESH,
        )

    exchange = [
        rows(0, tile_ref.at[2:4, 6:8], framed_ref.at[2:4, 0:2, 1], (lon, below)),
        rows(1, tile_ref.at[0:2, 7:8], framed_ref.at[0:2, 1:2, 1], (lon, below)),
        rows(2, tile_ref.at[0:4, 0:1], framed_ref.at[0:4, 10:11, 1], (lon, above)),
        rows(3, strips_ref.at[0:48], halo_ref.at[0:48], (right, lat)),
        rows(4, strips_ref.at[48:80], halo_ref.at[48:80], (left, lat)),
        rows(5, strips_ref.at[32:48], halo_ref.at[80:96], (right, below)),
        rows(6, strips_ref.at[64:80], halo_ref.at[96:112], (left, below)),
        rows(7, strips_ref.at[0:16], halo_ref.at[112:128], (right, above)),
        rows(8, strips_ref.at[48:64], halo_ref.at[128:144], (left, above)),
    ]
    for copy in reversed(exchange):
        copy.start()
    framed_ref[:, 2:10, 1] = embedded.reshape(4, 8, 16, D)
    for copy in exchange:
        copy.wait_recv()

    @pl.when(lat == 0)
    def _():
        halo_ref[80:112] = jnp.zeros((32, D), BF16)
        framed_ref[2:4, 1, 1] = jnp.zeros((2, 16, D), BF16)

    rim = jnp.dot(rim_ref[...], halo_ref[...], preferred_element_type=F32).astype(BF16)
    framed_ref[:, :, 0] = rim.reshape(4, 12, 16, D)

    planes = [framed_ref[i].reshape(384, D) for i in range(4)]
    span = 336

    def tap(a, c):
        plane = planes[(0 if a == 1 else 2) + (0 if c == 1 else 1)]
        base = 0 if a == 0 else 32
        return jnp.dot(
            plane[base : base + span], stride_weight_ref[3 * a + c], preferred_element_type=F32
        )

    before = tap(0, 0) + tap(1, 0) + tap(2, 0)
    here = tap(0, 1) + tap(1, 1) + tap(2, 1) + tap(0, 2) + tap(1, 2) + tap(2, 2)
    strided = pltpu.roll(before, 1, 0) + here + stride_bias_ref[...]
    coarse = gelu(strided).astype(BF16).astype(F32)
    at = lax.broadcasted_iota(jnp.int32, (span, D), 0)
    low = jnp.where(lat == 0, 40, 0)
    high = jnp.where(lat == ny - 1, 296, span)
    coarse = jnp.where((at >= low) & (at < high), coarse, 0.0)

    reach = 272

    def column(c):
        total = coarse[0:reach] * depth_weight_ref[c : c + 1]
        for a in (1, 2):
            total = total + coarse[32 * a : 32 * a + reach] * depth_weight_ref[3 * a + c : 3 * a + c + 1]
        return total

    mixed = (
        coarse[32 : 32 + reach]
        + column(1)
        + pltpu.roll(column(0), 1, 0)
        + pltpu.roll(column(2), reach - 1, 0)
    )
    mixed = mixed[:256].reshape(8, 2, 16, D)[:, 1]
    centre = mixed - jnp.mean(mixed, axis=-1, keepdims=True)
    variance = jnp.mean(centre * centre, axis=-1, keepdims=True)
    out_ref[...] = (centre * lax.rsqrt(variance + 1e-05) * gain_ref[...][None]).astype(BF16)

    for copy in exchange:
        copy.wait_send()
    send_code(pl.ds(1, tiles - 1), pl.ds(1, tiles - 1), 0, partners[0]).wait_send()
    send_values(pl.ds(1, tiles - 1), pl.ds(1, tiles - 1), 0, partners[0]).wait_send()


def physical(lons, lats):
    nc = 2
    nz = 4 if lons % 8 == 0 else 2
    return (lons // (nc * nz), nz, nc, lats)


def solution(mesh):
    dims = physical(mesh.shape["lon"], mesh.shape["lat"])
    tiles = mesh.shape["lon"] * mesh.shape["lat"]
    groups = tiles // GROUP
    vmem = pl.BlockSpec(memory_space=pltpu.VMEM)
    anywhere = pl.BlockSpec(memory_space=pl.ANY)
    strips, rims = strip_table(), rim_table()

    def on_device(
        obs_values,
        obs_offset,
        obs_cell,
        obs_slot,
        obs_count,
        embed_weight,
        embed_bias,
        stride_weight,
        stride_bias,
        depth_weight,
        norm_gain,
    ):
        return pl.pallas_call(
            functools.partial(kernel, dims),
            out_shape=jax.ShapeDtypeStruct((TLAT // 2, TLON // 2, D), BF16),
            in_specs=[
                anywhere,
                vmem,
                vmem,
                vmem,
                vmem,
                anywhere,
                vmem,
                anywhere,
                vmem,
                vmem,
                vmem,
                anywhere,
                anywhere,
            ],
            out_specs=vmem,
            scratch_shapes=[
                pltpu.VMEM((OBS_VARS, tiles, 256), BF16),
                pltpu.VMEM((2 * WIDTH * PITCH, 128), F32),
                pltpu.VMEM((tiles, WIDTH, 256), BF16),
                pltpu.VMEM((tiles, 1, 256), F32),
                pltpu.VMEM((tiles, WIDTH, 256), BF16),
                pltpu.VMEM((tiles, 1, 256), F32),
                pltpu.VMEM((SLOTS * WIDTH, GROUP * 256), BF16),
                pltpu.VMEM((CELLS, GROUP * 256), BF16),
                pltpu.VMEM((SLOTS * WIDTH, CELLS), F32),
                pltpu.VMEM((SLOTS * WIDTH, D), BF16),
                pltpu.VMEM((9, D, D), BF16),
                pltpu.VMEM((80, CELLS), BF16),
                pltpu.VMEM((768, 256), BF16),
                pltpu.VMEM((4, 8, 16, D), BF16),
                pltpu.VMEM((80, D), BF16),
                pltpu.VMEM((256, D), BF16),
                pltpu.VMEM((4, 12, 2, 16, D), BF16),
                pltpu.SemaphoreType.DMA((2,)),
                pltpu.SemaphoreType.DMA((2 * groups,)),
                pltpu.SemaphoreType.DMA((9,)),
                pltpu.SemaphoreType.DMA((9,)),
                pltpu.SemaphoreType.DMA((9,)),
            ],
            compiler_params=pltpu.CompilerParams(
                collective_id=0, has_side_effects=True, vmem_limit_bytes=60 << 20
            ),
        )(
            jnp.transpose(obs_values, (1, 0, 2)),
            obs_offset,
            obs_cell,
            obs_slot,
            obs_count,
            embed_weight,
            embed_bias[None],
            stride_weight,
            stride_bias[None],
            depth_weight,
            norm_gain[None],
            jnp.asarray(strips, BF16),
            jnp.asarray(rims, BF16),
        )

    placed = (
        P(("lon", "lat"), None, None),
        P(("lon", "lat"), None, None),
        P(("lon", "lat"), None),
        P(("lon", "lat"), None),
        P(("lon", "lat"), None),
        P(),
        P(),
        P(),
        P(),
        P(),
        P(),
    )
    return jax.shard_map(
        on_device, mesh=mesh, in_specs=placed, out_specs=P("lat", "lon", None), check_vma=False
    )
```

```python
import functools

import jax
import jax.numpy as jnp
import numpy as np
from jax import lax
from jax.experimental import pallas as pl
from jax.experimental.pallas import tpu as pltpu
from jax.sharding import PartitionSpec as P

MESH = pl.DeviceIdType.MESH
D = 256
OBS_VARS = 31
WIDTH = 32
SLOTS = 12
TLAT = 16
TLON = 32
CELLS = 512
GROUP = 8
BF16 = jnp.bfloat16
F32 = jnp.float32
PITCH = 136


def cell_number(row, col):
    return ((row % 2) * 2 + col % 2) * 128 + (row // 2) * 16 + col // 2


def strip_table():
    table = np.zeros((80, CELLS), np.float32)
    for row in range(TLAT):
        for i in range(3):
            table[row * 3 + i, cell_number(row, TLON - 3 + i)] = 1
        for i in range(2):
            table[48 + row * 2 + i, cell_number(row, i)] = 1
    return table


def rim_table():
    table = np.zeros((4, 12, 16, 256), np.float32)
    for plane in range(4):
        row_odd, col_odd = divmod(plane, 2)
        for p in range(-2, 9):
            row = 2 * p + row_odd
            if row < -3 or row > 17:
                continue
            for q in (-2, -1, 16):
                if q == -2 and not col_odd:
                    continue
                if q < 0:
                    i = 2 * q + col_odd + 3
                    if row < 0:
                        source = 80 + (row + 16) * 3 + i - 32
                    elif row < 16:
                        source = row * 3 + i
                    else:
                        source = 112 + (row - 16) * 3 + i
                    table[plane, p + 2, 16 + q, source] = 1
                else:
                    i = col_odd
                    if row < 0:
                        source = 96 + (row + 16) * 2 + i - 16
                    elif row < 16:
                        source = 48 + row * 2 + i
                    else:
                        source = 128 + (row - 16) * 2 + i
                    table[plane, p + 3, 0, source] = 1
    return table.reshape(4 * 12 * 16, 256)


def gelu(x):
    return 0.5 * x * (1.0 + jnp.tanh(0.7978845608028654 * (x + 0.044715 * (x * x * x))))


def scrambled(dims):
    nx, nz, nc, ny = dims
    offsets = [
        (dx, dz, dc, dy)
        for dx in range(nx)
        for dz in range(nz)
        for dc in range(nc)
        for dy in range(ny)
        if dx or dz or dc or dy
    ]
    return sorted(offsets, key=lambda o: (o[0] * 37 + o[1] * 59 + o[2] * 83 + o[3] * 101) % 127)


def kernel(
    dims,
    values_ref,
    offset_hbm,
    cell_hbm,
    slot_hbm,
    count_hbm,
    embed_weight_hbm,
    embed_bias_hbm,
    stride_weight_hbm,
    stride_bias_hbm,
    depth_weight_hbm,
    gain_hbm,
    strip_hbm,
    rim_hbm,
    out_ref,
    offset_ref,
    cell_ref,
    slot_ref,
    count_ref,
    embed_bias_ref,
    stride_bias_ref,
    depth_weight_ref,
    gain_ref,
    raw_ref,
    wide_ref,
    packed_ref,
    code_ref,
    recv_ref,
    recv_code_ref,
    spread_ref,
    hot_ref,
    total_ref,
    embed_weight_ref,
    stride_weight_ref,
    strip_ref,
    rim_ref,
    tile_ref,
    strips_ref,
    halo_ref,
    framed_ref,
    send_sem,
    recv_sem,
    first_sem,
    raw_sem,
    load_sem,
    halo_send_sem,
    halo_recv_sem,
):
    nx, nz, nc, ny = dims
    lons = nx * nz * nc
    tiles = lons * ny
    groups = tiles // GROUP
    lon, lat = lax.axis_index("lon"), lax.axis_index("lat")
    core = lon % nc
    z = (lon // nc) % nz
    x = lon // (nc * nz)

    def wrapped(value, size):
        return jnp.where(value >= size, value - size, value)

    at_x = [wrapped(x + i, nx) * (nz * nc) for i in range(nx)]
    at_z = [wrapped(z + i, nz) * nc for i in range(nz)]
    at_core = [wrapped(core + i, nc) for i in range(nc)]
    at_y = [wrapped(lat + i, ny) for i in range(ny)]
    order = scrambled(dims)
    partners = [(at_x[o[0]] + at_z[o[1]] + at_core[o[2]], at_y[o[3]]) for o in order]

    barrier = pltpu.get_barrier_semaphore()
    for partner in partners:
        pl.semaphore_signal(barrier, inc=1, device_id=partner, device_id_type=MESH)

    firsts = [
        pltpu.make_async_copy(source, target, first_sem.at[i])
        for i, (source, target) in enumerate(
            (
                (offset_hbm, offset_ref),
                (count_hbm, count_ref),
                (cell_hbm, cell_ref),
                (slot_hbm, slot_ref),
            )
        )
    ]
    for first in firsts:
        first.start()
    chunks = ((0, 8), (8, 16), (16, 24), (24, 31))
    raws = [
        pltpu.make_async_copy(
            values_ref.at[low:high], raw_ref.at[low:high], raw_sem.at[i]
        )
        for i, (low, high) in enumerate(chunks)
    ]
    for raw in raws:
        raw.start()
    halo_ref[...] = jnp.zeros_like(halo_ref)
    me = lon * ny + lat
    loads = [
        pltpu.make_async_copy(source, target, load_sem.at[i])
        for i, (source, target) in enumerate(
            (
                (embed_weight_hbm, embed_weight_ref),
                (stride_weight_hbm, stride_weight_ref),
                (strip_hbm, strip_ref),
                (rim_hbm, rim_ref),
                (embed_bias_hbm, embed_bias_ref),
                (stride_bias_hbm, stride_bias_ref),
                (depth_weight_hbm, depth_weight_ref),
                (gain_hbm, gain_ref),
            )
        )
    ]
    for first in firsts:
        first.wait()

    lane = lax.broadcasted_iota(jnp.int32, (tiles, tiles), 1)
    line = lax.broadcasted_iota(jnp.int32, (tiles, tiles), 0)
    count = jnp.sum(
        jnp.where(lane == line, count_ref[...].astype(F32), 0.0), axis=1, keepdims=True
    )
    position = lax.broadcasted_iota(jnp.int32, cell_ref.shape, 1).astype(F32)
    off_y, off_x = offset_ref[:, 0, :], offset_ref[:, 1, :]
    weight = jnp.where(position < count, jnp.exp(-2.0 * (off_y * off_y + off_x * off_x)), 0.0)
    cell = cell_ref[...]
    row, col = cell >> 5, cell & 31
    code = (
        slot_ref[...] * CELLS
        + (((row & 1) * 2 + (col & 1)) * 128 + (row >> 1) * 16 + (col >> 1))
    ).astype(F32)
    code_ref[:, 0, :] = code
    def widen(k, row):
        for h in range(2):
            start = (h * WIDTH + k) * PITCH
            wide_ref[start : start + tiles] = row[:, h * 128 : h * 128 + 128]

    widen(31, weight)
    for raw, (low, high) in zip(raws, chunks):
        raw.wait()
        for k in range(low, high):
            widen(k, raw_ref[k].astype(F32) * weight)

    def pack(target):
        halves = [
            wide_ref[pl.ds(target + h * WIDTH * PITCH, WIDTH, stride=PITCH), :] for h in range(2)
        ]
        return jnp.concatenate(halves, axis=1).astype(BF16)

    pl.semaphore_wait(barrier, tiles - 1)

    def send_values(source, target, sem, partner):
        return pltpu.make_async_remote_copy(
            packed_ref.at[source],
            recv_ref.at[target],
            send_sem.at[0],
            recv_sem.at[sem],
            device_id=partner,
            device_id_type=MESH,
        )

    def send_code(source, target, sem, partner):
        return pltpu.make_async_remote_copy(
            code_ref.at[source],
            recv_code_ref.at[target],
            send_sem.at[1],
            recv_sem.at[sem + groups],
            device_id=partner,
            device_id_type=MESH,
        )

    for i, partner in enumerate(partners, 1):
        to = partner[0] * ny + partner[1]
        packed_ref[i] = pack(to)
        send_code(to, i, i // GROUP, partner).start()
        send_values(i, i, i // GROUP, partner).start()

    for load in loads:
        load.start()
    recv_ref[0] = pack(me)
    recv_code_ref[0] = code_ref[me]
    total_ref[...] = jnp.zeros_like(total_ref)

    line16 = lax.broadcasted_iota(jnp.int32, (16, 256), 0).astype(F32).astype(BF16)

    def scatter(group):
        def build(i, carry):
            at = group * GROUP + i
            code = recv_code_ref[at]
            slot = jnp.floor(code * (1.0 / CELLS))
            cell = code - slot * CELLS
            half = jnp.where(cell >= 256, 1.0, 0.0)
            low = cell - 256.0 * half
            first = jnp.broadcast_to(jnp.where(half == 0.0, low, -1.0), (16, 256)).astype(BF16)
            second = jnp.broadcast_to(jnp.where(half == 1.0, low, -1.0), (16, 256)).astype(BF16)
            slot = jnp.broadcast_to(slot, (16, 256)).astype(BF16)
            packed = recv_ref[at]
            lanes = pl.ds(pl.multiple_of(i * 256, 256), 256)
            zero, one = jnp.zeros((16, 256), BF16), jnp.ones((16, 256), BF16)
            for s in range(SLOTS):
                mine = slot == s
                for h in range(2):
                    spread_ref[s * WIDTH + h * 16 : s * WIDTH + h * 16 + 16, lanes] = jnp.where(
                        mine, packed[h * 16 : h * 16 + 16], zero
                    )
            for h, wanted in enumerate((first, second)):
                for r in range(16):
                    at_row = h * 256 + r * 16
                    hot_ref[at_row : at_row + 16, lanes] = jnp.where(
                        wanted == line16 + (r * 16), one, zero
                    )
            return carry

        lax.fori_loop(0, GROUP, build, 0, unroll=True)
        total_ref[...] += lax.dot_general(
            spread_ref[...],
            hot_ref[...],
            (((1,), (1,)), ((), ())),
            preferred_element_type=F32,
        )

    def arrive(group, first, size):
        send_code(pl.ds(first, size), pl.ds(first, size), group, partners[0]).wait_recv()
        send_values(pl.ds(first, size), pl.ds(first, size), group, partners[0]).wait_recv()

    def group_step(group, carry):
        @pl.when(group == 0)
        def _():
            arrive(0, 1, GROUP - 1)

        @pl.when(group > 0)
        def _():
            arrive(group, group * GROUP, GROUP)

        scatter(group)
        return carry

    lax.fori_loop(0, groups, group_step, 0)

    for load in loads:
        load.wait()

    total = total_ref[...].reshape(SLOTS, WIDTH, CELLS)
    density = total[:, WIDTH - 1 :, :]
    variable = lax.broadcasted_iota(jnp.int32, (SLOTS, WIDTH, CELLS), 1)
    gridded = jnp.where(variable == WIDTH - 1, total, total / (1.0 + density))
    gridded = gridded.reshape(SLOTS * WIDTH, CELLS).astype(BF16)
    projected = lax.dot_general(
        gridded, embed_weight_ref[...], (((0,), (0,)), ((), ())), preferred_element_type=F32
    )
    embedded = gelu(projected + embed_bias_ref[...]).astype(BF16)
    tile_ref[...] = embedded.reshape(4, 8, 16, D)

    right, left = wrapped(lon + 1, lons), wrapped(lon + lons - 1, lons)
    below, above = wrapped(lat + 1, ny), wrapped(lat + ny - 1, ny)

    def rows(i, source, target, partner):
        return pltpu.make_async_remote_copy(
            source,
            target,
            halo_send_sem.at[i],
            halo_recv_sem.at[i],
            device_id=partner,
            device_id_type=MESH,
        )

    exchange = [
        rows(0, tile_ref.at[2:4, 6:8], framed_ref.at[2:4, 0:2, 1], (lon, below)),
        rows(1, tile_ref.at[0:2, 7:8], framed_ref.at[0:2, 1:2, 1], (lon, below)),
        rows(2, tile_ref.at[0:4, 0:1], framed_ref.at[0:4, 10:11, 1], (lon, above)),
        rows(3, strips_ref.at[0:48], halo_ref.at[0:48], (right, lat)),
        rows(4, strips_ref.at[48:80], halo_ref.at[48:80], (left, lat)),
        rows(5, strips_ref.at[32:48], halo_ref.at[80:96], (right, below)),
        rows(6, strips_ref.at[64:80], halo_ref.at[96:112], (left, below)),
        rows(7, strips_ref.at[0:16], halo_ref.at[112:128], (right, above)),
        rows(8, strips_ref.at[48:64], halo_ref.at[128:144], (left, above)),
    ]
    for copy in exchange[:3]:
        copy.start()
    strips_ref[...] = jnp.dot(strip_ref[...], embedded, preferred_element_type=F32).astype(BF16)
    for copy in exchange[3:]:
        copy.start()
    framed_ref[:, 2:10, 1] = embedded.reshape(4, 8, 16, D)
    for copy in exchange:
        copy.wait_recv()

    @pl.when(lat == 0)
    def _():
        halo_ref[80:112] = jnp.zeros((32, D), BF16)
        framed_ref[2:4, 1, 1] = jnp.zeros((2, 16, D), BF16)

    rim = jnp.dot(rim_ref[...], halo_ref[...], preferred_element_type=F32).astype(BF16)
    framed_ref[:, :, 0] = rim.reshape(4, 12, 16, D)

    planes = [framed_ref[i].reshape(384, D) for i in range(4)]
    span = 336

    def tap(a, c):
        plane = planes[(0 if a == 1 else 2) + (0 if c == 1 else 1)]
        base = 0 if a == 0 else 32
        return jnp.dot(
            plane[base : base + span], stride_weight_ref[3 * a + c], preferred_element_type=F32
        )

    before = tap(0, 0) + tap(1, 0) + tap(2, 0)
    here = tap(0, 1) + tap(1, 1) + tap(2, 1) + tap(0, 2) + tap(1, 2) + tap(2, 2)
    strided = pltpu.roll(before, 1, 0) + here + stride_bias_ref[...]
    coarse = gelu(strided).astype(BF16).astype(F32)
    at = lax.broadcasted_iota(jnp.int32, (span, D), 0)
    low = jnp.where(lat == 0, 40, 0)
    high = jnp.where(lat == ny - 1, 296, span)
    coarse = jnp.where((at >= low) & (at < high), coarse, 0.0)

    reach = 272

    def column(c):
        total = coarse[0:reach] * depth_weight_ref[c : c + 1]
        for a in (1, 2):
            total = total + coarse[32 * a : 32 * a + reach] * depth_weight_ref[3 * a + c : 3 * a + c + 1]
        return total

    mixed = (
        coarse[32 : 32 + reach]
        + column(1)
        + pltpu.roll(column(0), 1, 0)
        + pltpu.roll(column(2), reach - 1, 0)
    )
    mixed = mixed[:256].reshape(8, 2, 16, D)[:, 1]
    centre = mixed - jnp.mean(mixed, axis=-1, keepdims=True)
    variance = jnp.mean(centre * centre, axis=-1, keepdims=True)
    out_ref[...] = (centre * lax.rsqrt(variance + 1e-05) * gain_ref[...][None]).astype(BF16)

    for copy in exchange:
        copy.wait_send()
    send_code(pl.ds(1, tiles - 1), pl.ds(1, tiles - 1), 0, partners[0]).wait_send()
    send_values(pl.ds(1, tiles - 1), pl.ds(1, tiles - 1), 0, partners[0]).wait_send()


def physical(lons, lats):
    nc = 2
    nz = 4 if lons % 8 == 0 else 2
    return (lons // (nc * nz), nz, nc, lats)


def solution(mesh):
    dims = physical(mesh.shape["lon"], mesh.shape["lat"])
    tiles = mesh.shape["lon"] * mesh.shape["lat"]
    groups = tiles // GROUP
    vmem = pl.BlockSpec(memory_space=pltpu.VMEM)
    anywhere = pl.BlockSpec(memory_space=pl.ANY)
    strips, rims = strip_table(), rim_table()

    def on_device(
        obs_values,
        obs_offset,
        obs_cell,
        obs_slot,
        obs_count,
        embed_weight,
        embed_bias,
        stride_weight,
        stride_bias,
        depth_weight,
        norm_gain,
    ):
        return pl.pallas_call(
            functools.partial(kernel, dims),
            out_shape=jax.ShapeDtypeStruct((TLAT // 2, TLON // 2, D), BF16),
            in_specs=[anywhere] * 13,
            out_specs=vmem,
            scratch_shapes=[
                pltpu.VMEM((tiles, 2, 256), F32),
                pltpu.VMEM((tiles, 256), jnp.int32),
                pltpu.VMEM((tiles, 256), jnp.int32),
                pltpu.VMEM((1, tiles), jnp.int32),
                pltpu.VMEM((1, D), F32),
                pltpu.VMEM((1, D), F32),
                pltpu.VMEM((9, D), F32),
                pltpu.VMEM((1, D), F32),
                pltpu.VMEM((OBS_VARS, tiles, 256), BF16),
                pltpu.VMEM((2 * WIDTH * PITCH, 128), F32),
                pltpu.VMEM((tiles, WIDTH, 256), BF16),
                pltpu.VMEM((tiles, 1, 256), F32),
                pltpu.VMEM((tiles, WIDTH, 256), BF16),
                pltpu.VMEM((tiles, 1, 256), F32),
                pltpu.VMEM((SLOTS * WIDTH, GROUP * 256), BF16),
                pltpu.VMEM((CELLS, GROUP * 256), BF16),
                pltpu.VMEM((SLOTS * WIDTH, CELLS), F32),
                pltpu.VMEM((SLOTS * WIDTH, D), BF16),
                pltpu.VMEM((9, D, D), BF16),
                pltpu.VMEM((80, CELLS), BF16),
                pltpu.VMEM((768, 256), BF16),
                pltpu.VMEM((4, 8, 16, D), BF16),
                pltpu.VMEM((80, D), BF16),
                pltpu.VMEM((256, D), BF16),
                pltpu.VMEM((4, 12, 2, 16, D), BF16),
                pltpu.SemaphoreType.DMA((2,)),
                pltpu.SemaphoreType.DMA((2 * groups,)),
                pltpu.SemaphoreType.DMA((4,)),
                pltpu.SemaphoreType.DMA((4,)),
                pltpu.SemaphoreType.DMA((8,)),
                pltpu.SemaphoreType.DMA((9,)),
                pltpu.SemaphoreType.DMA((9,)),
            ],
            compiler_params=pltpu.CompilerParams(
                collective_id=0, has_side_effects=True, vmem_limit_bytes=60 << 20
            ),
        )(
            jnp.transpose(obs_values, (1, 0, 2)),
            obs_offset,
            obs_cell,
            obs_slot,
            obs_count,
            embed_weight,
            embed_bias[None],
            stride_weight,
            stride_bias[None],
            depth_weight,
            norm_gain[None],
            jnp.asarray(strips, BF16),
            jnp.asarray(rims, BF16),
        )

    placed = (
        P(("lon", "lat"), None, None),
        P(("lon", "lat"), None, None),
        P(("lon", "lat"), None),
        P(("lon", "lat"), None),
        P(("lon", "lat"), None),
        P(),
        P(),
        P(),
        P(),
        P(),
        P(),
    )
    return jax.shard_map(
        on_device, mesh=mesh, in_specs=placed, out_specs=P("lat", "lon", None), check_vma=False
    )
```

```python
import functools

import jax
import jax.numpy as jnp
import numpy as np
from jax import lax
from jax.experimental import pallas as pl
from jax.experimental.pallas import tpu as pltpu
from jax.sharding import PartitionSpec as P

MESH = pl.DeviceIdType.MESH
D = 256
OBS_VARS = 31
WIDTH = 32
SLOTS = 12
TLAT = 16
TLON = 32
CELLS = 512
GROUP = 8
BF16 = jnp.bfloat16
F32 = jnp.float32
PITCH = 136


def cell_number(row, col):
    return ((row % 2) * 2 + col % 2) * 128 + (row // 2) * 16 + col // 2


def strip_table():
    table = np.zeros((80, CELLS), np.float32)
    for row in range(TLAT):
        for i in range(3):
            table[row * 3 + i, cell_number(row, TLON - 3 + i)] = 1
        for i in range(2):
            table[48 + row * 2 + i, cell_number(row, i)] = 1
    return table


def rim_table():
    table = np.zeros((4, 12, 16, 256), np.float32)
    for plane in range(4):
        row_odd, col_odd = divmod(plane, 2)
        for p in range(-2, 9):
            row = 2 * p + row_odd
            if row < -3 or row > 17:
                continue
            for q in (-2, -1, 16):
                if q == -2 and not col_odd:
                    continue
                if q < 0:
                    i = 2 * q + col_odd + 3
                    if row < 0:
                        source = 80 + (row + 16) * 3 + i - 32
                    elif row < 16:
                        source = row * 3 + i
                    else:
                        source = 112 + (row - 16) * 3 + i
                    table[plane, p + 2, 16 + q, source] = 1
                else:
                    i = col_odd
                    if row < 0:
                        source = 96 + (row + 16) * 2 + i - 16
                    elif row < 16:
                        source = 48 + row * 2 + i
                    else:
                        source = 128 + (row - 16) * 2 + i
                    table[plane, p + 3, 0, source] = 1
    return table.reshape(4 * 12 * 16, 256)


def gelu(x):
    return 0.5 * x * (1.0 + jnp.tanh(0.7978845608028654 * (x + 0.044715 * (x * x * x))))


def scrambled(dims):
    nx, nz, nc, ny = dims
    offsets = [
        (dx, dz, dc, dy)
        for dx in range(nx)
        for dz in range(nz)
        for dc in range(nc)
        for dy in range(ny)
        if dx or dz or dc or dy
    ]
    return sorted(offsets, key=lambda o: (o[0] * 37 + o[1] * 59 + o[2] * 83 + o[3] * 101) % 127)


def kernel(
    dims,
    values_ref,
    offset_hbm,
    cell_hbm,
    slot_hbm,
    count_hbm,
    embed_weight_hbm,
    embed_bias_hbm,
    stride_weight_hbm,
    stride_bias_hbm,
    depth_weight_hbm,
    gain_hbm,
    strip_hbm,
    rim_hbm,
    out_ref,
    offset_ref,
    cell_ref,
    slot_ref,
    count_ref,
    embed_bias_ref,
    stride_bias_ref,
    depth_weight_ref,
    gain_ref,
    raw_ref,
    wide_ref,
    packed_ref,
    code_ref,
    recv_ref,
    recv_code_ref,
    spread_ref,
    hot_ref,
    total_ref,
    embed_weight_ref,
    stride_weight_ref,
    strip_ref,
    rim_ref,
    tile_ref,
    strips_ref,
    halo_ref,
    framed_ref,
    send_sem,
    recv_sem,
    first_sem,
    raw_sem,
    load_sem,
    halo_send_sem,
    halo_recv_sem,
):
    nx, nz, nc, ny = dims
    lons = nx * nz * nc
    tiles = lons * ny
    groups = tiles // GROUP
    lon, lat = lax.axis_index("lon"), lax.axis_index("lat")
    core = lon % nc
    z = (lon // nc) % nz
    x = lon // (nc * nz)

    def wrapped(value, size):
        return jnp.where(value >= size, value - size, value)

    at_x = [wrapped(x + i, nx) * (nz * nc) for i in range(nx)]
    at_z = [wrapped(z + i, nz) * nc for i in range(nz)]
    at_core = [wrapped(core + i, nc) for i in range(nc)]
    at_y = [wrapped(lat + i, ny) for i in range(ny)]
    order = scrambled(dims)
    partners = [(at_x[o[0]] + at_z[o[1]] + at_core[o[2]], at_y[o[3]]) for o in order]

    barrier = pltpu.get_barrier_semaphore()
    def reach(o):
        return min(o[0], nx - o[0]) + min(o[1], nz - o[1]) + min(o[3], ny - o[3])

    greeted = sorted(range(len(order)), key=lambda i: -reach(order[i]))
    for partner in [partners[i] for i in greeted]:
        pl.semaphore_signal(barrier, inc=1, device_id=partner, device_id_type=MESH)

    firsts = [
        pltpu.make_async_copy(source, target, first_sem.at[i])
        for i, (source, target) in enumerate(
            (
                (offset_hbm, offset_ref),
                (count_hbm, count_ref),
                (cell_hbm, cell_ref),
                (slot_hbm, slot_ref),
            )
        )
    ]
    for first in firsts:
        first.start()
    chunks = ((0, 8), (8, 16), (16, 24), (24, 31))
    raws = [
        pltpu.make_async_copy(
            values_ref.at[low:high], raw_ref.at[low:high], raw_sem.at[i]
        )
        for i, (low, high) in enumerate(chunks)
    ]
    for raw in raws:
        raw.start()
    halo_ref[...] = jnp.zeros_like(halo_ref)
    me = lon * ny + lat
    loads = [
        pltpu.make_async_copy(source, target, load_sem.at[i])
        for i, (source, target) in enumerate(
            (
                (embed_weight_hbm, embed_weight_ref),
                (stride_weight_hbm, stride_weight_ref),
                (strip_hbm, strip_ref),
                (rim_hbm, rim_ref),
                (embed_bias_hbm, embed_bias_ref),
                (stride_bias_hbm, stride_bias_ref),
                (depth_weight_hbm, depth_weight_ref),
                (gain_hbm, gain_ref),
            )
        )
    ]
    for first in firsts:
        first.wait()

    lane = lax.broadcasted_iota(jnp.int32, (tiles, tiles), 1)
    line = lax.broadcasted_iota(jnp.int32, (tiles, tiles), 0)
    count = jnp.sum(
        jnp.where(lane == line, count_ref[...].astype(F32), 0.0), axis=1, keepdims=True
    )
    position = lax.broadcasted_iota(jnp.int32, cell_ref.shape, 1).astype(F32)
    off_y, off_x = offset_ref[:, 0, :], offset_ref[:, 1, :]
    weight = jnp.where(position < count, jnp.exp(-2.0 * (off_y * off_y + off_x * off_x)), 0.0)
    cell = cell_ref[...]
    row, col = cell >> 5, cell & 31
    code = (
        slot_ref[...] * CELLS
        + (((row & 1) * 2 + (col & 1)) * 128 + (row >> 1) * 16 + (col >> 1))
    ).astype(F32)
    code_ref[:, 0, :] = code
    def widen(k, row):
        for h in range(2):
            start = (h * WIDTH + k) * PITCH
            wide_ref[start : start + tiles] = row[:, h * 128 : h * 128 + 128]

    widen(31, weight)
    for raw, (low, high) in zip(raws, chunks):
        raw.wait()
        for k in range(low, high):
            widen(k, raw_ref[k].astype(F32) * weight)

    def pack(target):
        halves = [
            wide_ref[pl.ds(target + h * WIDTH * PITCH, WIDTH, stride=PITCH), :] for h in range(2)
        ]
        return jnp.concatenate(halves, axis=1).astype(BF16)

    pl.semaphore_wait(barrier, tiles - 1)

    def send_values(source, target, sem, partner):
        return pltpu.make_async_remote_copy(
            packed_ref.at[source],
            recv_ref.at[target],
            send_sem.at[0],
            recv_sem.at[sem],
            device_id=partner,
            device_id_type=MESH,
        )

    def send_code(source, target, sem, partner):
        return pltpu.make_async_remote_copy(
            code_ref.at[source],
            recv_code_ref.at[target],
            send_sem.at[1],
            recv_sem.at[sem + groups],
            device_id=partner,
            device_id_type=MESH,
        )

    for i, partner in enumerate(partners, 1):
        to = partner[0] * ny + partner[1]
        packed_ref[i] = pack(to)
        send_code(to, i, i // GROUP, partner).start()
        send_values(i, i, i // GROUP, partner).start()

    for load in loads:
        load.start()
    recv_ref[0] = pack(me)
    recv_code_ref[0] = code_ref[me]
    total_ref[...] = jnp.zeros_like(total_ref)

    line16 = lax.broadcasted_iota(jnp.int32, (16, 256), 0).astype(F32).astype(BF16)

    def scatter(group):
        def build(i, carry):
            at = group * GROUP + i
            code = recv_code_ref[at]
            slot = jnp.floor(code * (1.0 / CELLS))
            cell = code - slot * CELLS
            half = jnp.where(cell >= 256, 1.0, 0.0)
            low = cell - 256.0 * half
            first = jnp.broadcast_to(jnp.where(half == 0.0, low, -1.0), (16, 256)).astype(BF16)
            second = jnp.broadcast_to(jnp.where(half == 1.0, low, -1.0), (16, 256)).astype(BF16)
            slot = jnp.broadcast_to(slot, (16, 256)).astype(BF16)
            packed = recv_ref[at]
            lanes = pl.ds(pl.multiple_of(i * 256, 256), 256)
            zero, one = jnp.zeros((16, 256), BF16), jnp.ones((16, 256), BF16)
            for s in range(SLOTS):
                mine = slot == s
                for h in range(2):
                    spread_ref[s * WIDTH + h * 16 : s * WIDTH + h * 16 + 16, lanes] = jnp.where(
                        mine, packed[h * 16 : h * 16 + 16], zero
                    )
            for h, wanted in enumerate((first, second)):
                for r in range(16):
                    at_row = h * 256 + r * 16
                    hot_ref[at_row : at_row + 16, lanes] = jnp.where(
                        wanted == line16 + (r * 16), one, zero
                    )
            return carry

        lax.fori_loop(0, GROUP, build, 0, unroll=True)
        total_ref[...] += lax.dot_general(
            spread_ref[...],
            hot_ref[...],
            (((1,), (1,)), ((), ())),
            preferred_element_type=F32,
        )

    def arrive(group, first, size):
        send_code(pl.ds(first, size), pl.ds(first, size), group, partners[0]).wait_recv()
        send_values(pl.ds(first, size), pl.ds(first, size), group, partners[0]).wait_recv()

    def group_step(group, carry):
        @pl.when(group == 0)
        def _():
            arrive(0, 1, GROUP - 1)

        @pl.when(group > 0)
        def _():
            arrive(group, group * GROUP, GROUP)

        scatter(group)
        return carry

    lax.fori_loop(0, groups, group_step, 0)

    for load in loads:
        load.wait()

    total = total_ref[...].reshape(SLOTS, WIDTH, CELLS)
    density = total[:, WIDTH - 1 :, :]
    variable = lax.broadcasted_iota(jnp.int32, (SLOTS, WIDTH, CELLS), 1)
    gridded = jnp.where(variable == WIDTH - 1, total, total / (1.0 + density))
    gridded = gridded.reshape(SLOTS * WIDTH, CELLS).astype(BF16)
    projected = lax.dot_general(
        gridded, embed_weight_ref[...], (((0,), (0,)), ((), ())), preferred_element_type=F32
    )
    embedded = gelu(projected + embed_bias_ref[...]).astype(BF16)
    tile_ref[...] = embedded.reshape(4, 8, 16, D)

    right, left = wrapped(lon + 1, lons), wrapped(lon + lons - 1, lons)
    below, above = wrapped(lat + 1, ny), wrapped(lat + ny - 1, ny)

    def rows(i, source, target, partner):
        return pltpu.make_async_remote_copy(
            source,
            target,
            halo_send_sem.at[i],
            halo_recv_sem.at[i],
            device_id=partner,
            device_id_type=MESH,
        )

    exchange = [
        rows(0, tile_ref.at[2:4, 6:8], framed_ref.at[2:4, 0:2, 1], (lon, below)),
        rows(1, tile_ref.at[0:2, 7:8], framed_ref.at[0:2, 1:2, 1], (lon, below)),
        rows(2, tile_ref.at[0:4, 0:1], framed_ref.at[0:4, 10:11, 1], (lon, above)),
        rows(3, strips_ref.at[0:48], halo_ref.at[0:48], (right, lat)),
        rows(4, strips_ref.at[48:80], halo_ref.at[48:80], (left, lat)),
        rows(5, strips_ref.at[32:48], halo_ref.at[80:96], (right, below)),
        rows(6, strips_ref.at[64:80], halo_ref.at[96:112], (left, below)),
        rows(7, strips_ref.at[0:16], halo_ref.at[112:128], (right, above)),
        rows(8, strips_ref.at[48:64], halo_ref.at[128:144], (left, above)),
    ]
    for copy in exchange[:3]:
        copy.start()
    strips_ref[...] = jnp.dot(strip_ref[...], embedded, preferred_element_type=F32).astype(BF16)
    for copy in exchange[3:]:
        copy.start()
    framed_ref[:, 2:10, 1] = embedded.reshape(4, 8, 16, D)
    for copy in exchange:
        copy.wait_recv()

    @pl.when(lat == 0)
    def _():
        halo_ref[80:112] = jnp.zeros((32, D), BF16)
        framed_ref[2:4, 1, 1] = jnp.zeros((2, 16, D), BF16)

    rim = jnp.dot(rim_ref[...], halo_ref[...], preferred_element_type=F32).astype(BF16)
    framed_ref[:, :, 0] = rim.reshape(4, 12, 16, D)

    planes = [framed_ref[i].reshape(384, D) for i in range(4)]
    span = 336

    def tap(a, c):
        plane = planes[(0 if a == 1 else 2) + (0 if c == 1 else 1)]
        base = 0 if a == 0 else 32
        return jnp.dot(
            plane[base : base + span], stride_weight_ref[3 * a + c], preferred_element_type=F32
        )

    before = tap(0, 0) + tap(1, 0) + tap(2, 0)
    here = tap(0, 1) + tap(1, 1) + tap(2, 1) + tap(0, 2) + tap(1, 2) + tap(2, 2)
    strided = pltpu.roll(before, 1, 0) + here + stride_bias_ref[...]
    coarse = gelu(strided).astype(BF16).astype(F32)
    at = lax.broadcasted_iota(jnp.int32, (span, D), 0)
    low = jnp.where(lat == 0, 40, 0)
    high = jnp.where(lat == ny - 1, 296, span)
    coarse = jnp.where((at >= low) & (at < high), coarse, 0.0)

    reach = 272

    def column(c):
        total = coarse[0:reach] * depth_weight_ref[c : c + 1]
        for a in (1, 2):
            total = total + coarse[32 * a : 32 * a + reach] * depth_weight_ref[3 * a + c : 3 * a + c + 1]
        return total

    mixed = (
        coarse[32 : 32 + reach]
        + column(1)
        + pltpu.roll(column(0), 1, 0)
        + pltpu.roll(column(2), reach - 1, 0)
    )
    mixed = mixed[:256].reshape(8, 2, 16, D)[:, 1]
    centre = mixed - jnp.mean(mixed, axis=-1, keepdims=True)
    variance = jnp.mean(centre * centre, axis=-1, keepdims=True)
    out_ref[...] = (centre * lax.rsqrt(variance + 1e-05) * gain_ref[...][None]).astype(BF16)

    for copy in exchange:
        copy.wait_send()
    send_code(pl.ds(1, tiles - 1), pl.ds(1, tiles - 1), 0, partners[0]).wait_send()
    send_values(pl.ds(1, tiles - 1), pl.ds(1, tiles - 1), 0, partners[0]).wait_send()


def physical(lons, lats):
    nc = 2
    nz = 4 if lons % 8 == 0 else 2
    return (lons // (nc * nz), nz, nc, lats)


def solution(mesh):
    dims = physical(mesh.shape["lon"], mesh.shape["lat"])
    tiles = mesh.shape["lon"] * mesh.shape["lat"]
    groups = tiles // GROUP
    vmem = pl.BlockSpec(memory_space=pltpu.VMEM)
    anywhere = pl.BlockSpec(memory_space=pl.ANY)
    strips, rims = strip_table(), rim_table()

    def on_device(
        obs_values,
        obs_offset,
        obs_cell,
        obs_slot,
        obs_count,
        embed_weight,
        embed_bias,
        stride_weight,
        stride_bias,
        depth_weight,
        norm_gain,
    ):
        return pl.pallas_call(
            functools.partial(kernel, dims),
            out_shape=jax.ShapeDtypeStruct((TLAT // 2, TLON // 2, D), BF16),
            in_specs=[anywhere] * 13,
            out_specs=vmem,
            scratch_shapes=[
                pltpu.VMEM((tiles, 2, 256), F32),
                pltpu.VMEM((tiles, 256), jnp.int32),
                pltpu.VMEM((tiles, 256), jnp.int32),
                pltpu.VMEM((1, tiles), jnp.int32),
                pltpu.VMEM((1, D), F32),
                pltpu.VMEM((1, D), F32),
                pltpu.VMEM((9, D), F32),
                pltpu.VMEM((1, D), F32),
                pltpu.VMEM((OBS_VARS, tiles, 256), BF16),
                pltpu.VMEM((2 * WIDTH * PITCH, 128), F32),
                pltpu.VMEM((tiles, WIDTH, 256), BF16),
                pltpu.VMEM((tiles, 1, 256), F32),
                pltpu.VMEM((tiles, WIDTH, 256), BF16),
                pltpu.VMEM((tiles, 1, 256), F32),
                pltpu.VMEM((SLOTS * WIDTH, GROUP * 256), BF16),
                pltpu.VMEM((CELLS, GROUP * 256), BF16),
                pltpu.VMEM((SLOTS * WIDTH, CELLS), F32),
                pltpu.VMEM((SLOTS * WIDTH, D), BF16),
                pltpu.VMEM((9, D, D), BF16),
                pltpu.VMEM((80, CELLS), BF16),
                pltpu.VMEM((768, 256), BF16),
                pltpu.VMEM((4, 8, 16, D), BF16),
                pltpu.VMEM((80, D), BF16),
                pltpu.VMEM((256, D), BF16),
                pltpu.VMEM((4, 12, 2, 16, D), BF16),
                pltpu.SemaphoreType.DMA((2,)),
                pltpu.SemaphoreType.DMA((2 * groups,)),
                pltpu.SemaphoreType.DMA((4,)),
                pltpu.SemaphoreType.DMA((4,)),
                pltpu.SemaphoreType.DMA((8,)),
                pltpu.SemaphoreType.DMA((9,)),
                pltpu.SemaphoreType.DMA((9,)),
            ],
            compiler_params=pltpu.CompilerParams(
                collective_id=0, has_side_effects=True, vmem_limit_bytes=60 << 20
            ),
        )(
            jnp.transpose(obs_values, (1, 0, 2)),
            obs_offset,
            obs_cell,
            obs_slot,
            obs_count,
            embed_weight,
            embed_bias[None],
            stride_weight,
            stride_bias[None],
            depth_weight,
            norm_gain[None],
            jnp.asarray(strips, BF16),
            jnp.asarray(rims, BF16),
        )

    placed = (
        P(("lon", "lat"), None, None),
        P(("lon", "lat"), None, None),
        P(("lon", "lat"), None),
        P(("lon", "lat"), None),
        P(("lon", "lat"), None),
        P(),
        P(),
        P(),
        P(),
        P(),
        P(),
    )
    return jax.shard_map(
        on_device, mesh=mesh, in_specs=placed, out_specs=P("lat", "lon", None), check_vma=False
    )
```

```python
import functools

import jax
import jax.numpy as jnp
import numpy as np
from jax import lax
from jax.experimental import pallas as pl
from jax.experimental.pallas import tpu as pltpu
from jax.sharding import PartitionSpec as P

MESH = pl.DeviceIdType.MESH
D = 256
OBS_VARS = 31
WIDTH = 32
SLOTS = 12
TLAT = 16
TLON = 32
CELLS = 512
GROUP = 8
BF16 = jnp.bfloat16
F32 = jnp.float32
PITCH = 136


def cell_number(row, col):
    return ((row % 2) * 2 + col % 2) * 128 + (row // 2) * 16 + col // 2


def strip_table():
    table = np.zeros((80, CELLS), np.float32)
    for row in range(TLAT):
        for i in range(3):
            table[row * 3 + i, cell_number(row, TLON - 3 + i)] = 1
        for i in range(2):
            table[48 + row * 2 + i, cell_number(row, i)] = 1
    return table


def rim_table():
    table = np.zeros((4, 12, 16, 256), np.float32)
    for plane in range(4):
        row_odd, col_odd = divmod(plane, 2)
        for p in range(-2, 9):
            row = 2 * p + row_odd
            if row < -3 or row > 17:
                continue
            for q in (-2, -1, 16):
                if q == -2 and not col_odd:
                    continue
                if q < 0:
                    i = 2 * q + col_odd + 3
                    if row < 0:
                        source = 80 + (row + 16) * 3 + i - 32
                    elif row < 16:
                        source = row * 3 + i
                    else:
                        source = 112 + (row - 16) * 3 + i
                    table[plane, p + 2, 16 + q, source] = 1
                else:
                    i = col_odd
                    if row < 0:
                        source = 96 + (row + 16) * 2 + i - 16
                    elif row < 16:
                        source = 48 + row * 2 + i
                    else:
                        source = 128 + (row - 16) * 2 + i
                    table[plane, p + 3, 0, source] = 1
    return table.reshape(4 * 12 * 16, 256)


def gelu(x):
    return 0.5 * x * (1.0 + jnp.tanh(0.7978845608028654 * (x + 0.044715 * (x * x * x))))


def scrambled(dims):
    nx, nz, nc, ny = dims
    offsets = [
        (dx, dz, dc, dy)
        for dx in range(nx)
        for dz in range(nz)
        for dc in range(nc)
        for dy in range(ny)
        if dx or dz or dc or dy
    ]
    return sorted(offsets, key=lambda o: (o[0] * 37 + o[1] * 59 + o[2] * 83 + o[3] * 101) % 127)


def kernel(
    dims,
    values_ref,
    offset_hbm,
    cell_hbm,
    slot_hbm,
    count_hbm,
    embed_weight_hbm,
    embed_bias_hbm,
    stride_weight_hbm,
    stride_bias_hbm,
    depth_weight_hbm,
    gain_hbm,
    strip_hbm,
    rim_hbm,
    out_ref,
    offset_ref,
    cell_ref,
    slot_ref,
    count_ref,
    embed_bias_ref,
    stride_bias_ref,
    depth_weight_ref,
    gain_ref,
    raw_ref,
    wide_ref,
    packed_ref,
    code_ref,
    recv_ref,
    recv_code_ref,
    spread_ref,
    hot_ref,
    total_ref,
    embed_weight_ref,
    stride_weight_ref,
    strip_ref,
    rim_ref,
    tile_ref,
    strips_ref,
    halo_ref,
    framed_ref,
    send_sem,
    recv_sem,
    first_sem,
    raw_sem,
    load_sem,
    halo_send_sem,
    halo_recv_sem,
):
    nx, nz, nc, ny = dims
    lons = nx * nz * nc
    tiles = lons * ny
    groups = tiles // GROUP
    lon, lat = lax.axis_index("lon"), lax.axis_index("lat")
    core = lon % nc
    z = (lon // nc) % nz
    x = lon // (nc * nz)

    def wrapped(value, size):
        return jnp.where(value >= size, value - size, value)

    at_x = [wrapped(x + i, nx) * (nz * nc) for i in range(nx)]
    at_z = [wrapped(z + i, nz) * nc for i in range(nz)]
    at_core = [wrapped(core + i, nc) for i in range(nc)]
    at_y = [wrapped(lat + i, ny) for i in range(ny)]
    order = scrambled(dims)
    partners = [(at_x[o[0]] + at_z[o[1]] + at_core[o[2]], at_y[o[3]]) for o in order]

    barrier = pltpu.get_barrier_semaphore()
    def reach(o):
        return min(o[0], nx - o[0]) + min(o[1], nz - o[1]) + min(o[3], ny - o[3])

    greeted = sorted(range(len(order)), key=lambda i: -reach(order[i]))
    for partner in [partners[i] for i in greeted]:
        pl.semaphore_signal(barrier, inc=1, device_id=partner, device_id_type=MESH)

    firsts = [
        pltpu.make_async_copy(source, target, first_sem.at[i])
        for i, (source, target) in enumerate(
            (
                (offset_hbm, offset_ref),
                (count_hbm, count_ref),
                (cell_hbm, cell_ref),
                (slot_hbm, slot_ref),
            )
        )
    ]
    for first in firsts:
        first.start()
    chunks = ((0, 8), (8, 16), (16, 24), (24, 31))
    raws = [
        pltpu.make_async_copy(
            values_ref.at[low:high], raw_ref.at[low:high], raw_sem.at[i]
        )
        for i, (low, high) in enumerate(chunks)
    ]
    for raw in raws:
        raw.start()
    halo_ref[...] = jnp.zeros_like(halo_ref)
    me = lon * ny + lat
    loads = [
        pltpu.make_async_copy(source, target, load_sem.at[i])
        for i, (source, target) in enumerate(
            (
                (embed_weight_hbm, embed_weight_ref),
                (stride_weight_hbm, stride_weight_ref),
                (strip_hbm, strip_ref),
                (rim_hbm, rim_ref),
                (embed_bias_hbm, embed_bias_ref),
                (stride_bias_hbm, stride_bias_ref),
                (depth_weight_hbm, depth_weight_ref),
                (gain_hbm, gain_ref),
            )
        )
    ]
    for first in firsts:
        first.wait()

    lane = lax.broadcasted_iota(jnp.int32, (tiles, tiles), 1)
    line = lax.broadcasted_iota(jnp.int32, (tiles, tiles), 0)
    count = jnp.sum(
        jnp.where(lane == line, count_ref[...].astype(F32), 0.0), axis=1, keepdims=True
    )
    position = lax.broadcasted_iota(jnp.int32, cell_ref.shape, 1).astype(F32)
    off_y, off_x = offset_ref[:, 0, :], offset_ref[:, 1, :]
    weight = jnp.where(position < count, jnp.exp(-2.0 * (off_y * off_y + off_x * off_x)), 0.0)
    cell = cell_ref[...]
    row, col = cell >> 5, cell & 31
    code = (
        slot_ref[...] * CELLS
        + (((row & 1) * 2 + (col & 1)) * 128 + (row >> 1) * 16 + (col >> 1))
    ).astype(F32)
    code_ref[:, 0, :] = code
    def widen(k, row):
        for h in range(2):
            start = (h * WIDTH + k) * PITCH
            wide_ref[start : start + tiles] = row[:, h * 128 : h * 128 + 128]

    widen(31, weight)
    for raw, (low, high) in zip(raws, chunks):
        raw.wait()
        for k in range(low, high):
            widen(k, raw_ref[k].astype(F32) * weight)

    def pack(target):
        halves = [
            wide_ref[pl.ds(target + h * WIDTH * PITCH, WIDTH, stride=PITCH), :] for h in range(2)
        ]
        return jnp.concatenate(halves, axis=1).astype(BF16)

    pl.semaphore_wait(barrier, tiles - 1)

    def send_values(source, target, sem, partner):
        return pltpu.make_async_remote_copy(
            packed_ref.at[source],
            recv_ref.at[target],
            send_sem.at[0],
            recv_sem.at[sem],
            device_id=partner,
            device_id_type=MESH,
        )

    def send_code(source, target, sem, partner):
        return pltpu.make_async_remote_copy(
            code_ref.at[source],
            recv_code_ref.at[target],
            send_sem.at[1],
            recv_sem.at[sem + groups],
            device_id=partner,
            device_id_type=MESH,
        )

    for i, partner in enumerate(partners, 1):
        to = partner[0] * ny + partner[1]
        packed_ref[i] = pack(to)
        send_code(to, i, i // GROUP, partner).start()
        send_values(i, i, i // GROUP, partner).start()

    for load in loads:
        load.start()
    recv_ref[0] = pack(me)
    recv_code_ref[0] = code_ref[me]
    total_ref[...] = jnp.zeros_like(total_ref)

    line16 = lax.broadcasted_iota(jnp.int32, (16, 256), 0).astype(F32).astype(BF16)

    def scatter(group):
        def build(i, carry):
            at = group * GROUP + i
            code = recv_code_ref[at]
            slot = jnp.floor(code * (1.0 / CELLS))
            cell = code - slot * CELLS
            half = jnp.where(cell >= 256, 1.0, 0.0)
            low = cell - 256.0 * half
            first = jnp.broadcast_to(jnp.where(half == 0.0, low, -1.0), (16, 256)).astype(BF16)
            second = jnp.broadcast_to(jnp.where(half == 1.0, low, -1.0), (16, 256)).astype(BF16)
            slot = jnp.broadcast_to(slot, (16, 256)).astype(BF16)
            packed = recv_ref[at]
            lanes = pl.ds(pl.multiple_of(i * 256, 256), 256)
            zero, one = jnp.zeros((16, 256), BF16), jnp.ones((16, 256), BF16)
            for s in range(SLOTS):
                mine = slot == s
                for h in range(2):
                    spread_ref[s * WIDTH + h * 16 : s * WIDTH + h * 16 + 16, lanes] = jnp.where(
                        mine, packed[h * 16 : h * 16 + 16], zero
                    )
            for h, wanted in enumerate((first, second)):
                for r in range(16):
                    at_row = h * 256 + r * 16
                    hot_ref[at_row : at_row + 16, lanes] = jnp.where(
                        wanted == line16 + (r * 16), one, zero
                    )
            return carry

        lax.fori_loop(0, GROUP, build, 0, unroll=True)
        total_ref[...] += lax.dot_general(
            spread_ref[...],
            hot_ref[...],
            (((1,), (1,)), ((), ())),
            preferred_element_type=F32,
        )

    def arrive(group, first, size):
        send_code(pl.ds(first, size), pl.ds(first, size), group, partners[0]).wait_recv()
        send_values(pl.ds(first, size), pl.ds(first, size), group, partners[0]).wait_recv()

    def group_step(group, carry):
        @pl.when(group == 0)
        def _():
            arrive(0, 1, GROUP - 1)

        @pl.when(group > 0)
        def _():
            arrive(group, group * GROUP, GROUP)

        scatter(group)
        return carry

    lax.fori_loop(0, groups, group_step, 0)

    for load in loads:
        load.wait()

    total = total_ref[...].reshape(SLOTS, WIDTH, CELLS)
    density = total[:, WIDTH - 1 :, :]
    variable = lax.broadcasted_iota(jnp.int32, (SLOTS, WIDTH, CELLS), 1)
    gridded = jnp.where(variable == WIDTH - 1, total, total / (1.0 + density))
    gridded = gridded.reshape(SLOTS * WIDTH, CELLS).astype(BF16)
    projected = lax.dot_general(
        gridded, embed_weight_ref[...], (((0,), (0,)), ((), ())), preferred_element_type=F32
    )
    embedded = gelu(projected + embed_bias_ref[...]).astype(BF16)
    tile_ref[...] = embedded.reshape(4, 8, 16, D)

    right, left = wrapped(lon + 1, lons), wrapped(lon + lons - 1, lons)
    below, above = wrapped(lat + 1, ny), wrapped(lat + ny - 1, ny)

    def rows(i, source, target, partner):
        return pltpu.make_async_remote_copy(
            source,
            target,
            halo_send_sem.at[i],
            halo_recv_sem.at[i],
            device_id=partner,
            device_id_type=MESH,
        )

    exchange = [
        rows(0, tile_ref.at[2:4, 6:8], framed_ref.at[2:4, 0:2, 1], (lon, below)),
        rows(1, tile_ref.at[0:2, 7:8], framed_ref.at[0:2, 1:2, 1], (lon, below)),
        rows(2, tile_ref.at[0:4, 0:1], framed_ref.at[0:4, 10:11, 1], (lon, above)),
        rows(3, strips_ref.at[0:48], halo_ref.at[0:48], (right, lat)),
        rows(4, strips_ref.at[48:80], halo_ref.at[48:80], (left, lat)),
        rows(5, strips_ref.at[32:48], halo_ref.at[80:96], (right, below)),
        rows(6, strips_ref.at[64:80], halo_ref.at[96:112], (left, below)),
        rows(7, strips_ref.at[0:16], halo_ref.at[112:128], (right, above)),
        rows(8, strips_ref.at[48:64], halo_ref.at[128:144], (left, above)),
    ]
    for copy in exchange[:3]:
        copy.start()
    strips_ref[...] = jnp.dot(strip_ref[...], embedded, preferred_element_type=F32).astype(BF16)
    for copy in exchange[3:]:
        copy.start()
    framed_ref[:, 2:10, 1] = embedded.reshape(4, 8, 16, D)
    for copy in exchange:
        copy.wait_recv()

    @pl.when(lat == 0)
    def _():
        halo_ref[80:112] = jnp.zeros((32, D), BF16)
        framed_ref[2:4, 1, 1] = jnp.zeros((2, 16, D), BF16)

    rim = jnp.dot(rim_ref[...], halo_ref[...], preferred_element_type=F32).astype(BF16)
    framed_ref[:, :, 0] = rim.reshape(4, 12, 16, D)

    planes = [framed_ref[i].reshape(384, D) for i in range(4)]
    span = 336

    def tap(a, c):
        plane = planes[(0 if a == 1 else 2) + (0 if c == 1 else 1)]
        base = 0 if a == 0 else 32
        return jnp.dot(
            plane[base : base + span], stride_weight_ref[3 * a + c], preferred_element_type=F32
        )

    before = tap(0, 0) + tap(1, 0) + tap(2, 0)
    here = tap(0, 1) + tap(1, 1) + tap(2, 1) + tap(0, 2) + tap(1, 2) + tap(2, 2)
    strided = pltpu.roll(before, 1, 0) + here + stride_bias_ref[...]
    coarse = gelu(strided).astype(BF16).astype(F32)
    at = lax.broadcasted_iota(jnp.int32, (span, D), 0)
    low = jnp.where(lat == 0, 40, 0)
    high = jnp.where(lat == ny - 1, 296, span)
    coarse = jnp.where((at >= low) & (at < high), coarse, 0.0)

    reach = 272

    def column(c):
        total = coarse[0:reach] * depth_weight_ref[c : c + 1]
        for a in (1, 2):
            total = total + coarse[32 * a : 32 * a + reach] * depth_weight_ref[3 * a + c : 3 * a + c + 1]
        return total

    mixed = (
        coarse[32 : 32 + reach]
        + column(1)
        + pltpu.roll(column(0), 1, 0)
        + pltpu.roll(column(2), reach - 1, 0)
    )
    mixed = mixed[:256].reshape(8, 2, 16, D)[:, 1]
    centre = mixed - jnp.mean(mixed, axis=-1, keepdims=True)
    variance = jnp.mean(centre * centre, axis=-1, keepdims=True)
    out_ref[...] = (centre * lax.rsqrt(variance + 1e-05) * gain_ref[...][None]).astype(BF16)

    for copy in exchange:
        copy.wait_send()
    send_code(pl.ds(1, tiles - 1), pl.ds(1, tiles - 1), 0, partners[0]).wait_send()
    send_values(pl.ds(1, tiles - 1), pl.ds(1, tiles - 1), 0, partners[0]).wait_send()


def physical(lons, lats):
    nc = 2
    nz = 4 if lons % 8 == 0 else 2
    return (lons // (nc * nz), nz, nc, lats)


def solution(mesh):
    dims = physical(mesh.shape["lon"], mesh.shape["lat"])
    tiles = mesh.shape["lon"] * mesh.shape["lat"]
    groups = tiles // GROUP
    vmem = pl.BlockSpec(memory_space=pltpu.VMEM)
    anywhere = pl.BlockSpec(memory_space=pl.ANY)
    strips, rims = strip_table(), rim_table()

    def on_device(
        obs_values,
        obs_offset,
        obs_cell,
        obs_slot,
        obs_count,
        embed_weight,
        embed_bias,
        stride_weight,
        stride_bias,
        depth_weight,
        norm_gain,
    ):
        return pl.pallas_call(
            functools.partial(kernel, dims),
            out_shape=pltpu.VMEM((TLAT // 2, TLON // 2, D), BF16),
            in_specs=[anywhere] * 13,
            out_specs=vmem,
            scratch_shapes=[
                pltpu.VMEM((tiles, 2, 256), F32),
                pltpu.VMEM((tiles, 256), jnp.int32),
                pltpu.VMEM((tiles, 256), jnp.int32),
                pltpu.VMEM((1, tiles), jnp.int32),
                pltpu.VMEM((1, D), F32),
                pltpu.VMEM((1, D), F32),
                pltpu.VMEM((9, D), F32),
                pltpu.VMEM((1, D), F32),
                pltpu.VMEM((OBS_VARS, tiles, 256), BF16),
                pltpu.VMEM((2 * WIDTH * PITCH, 128), F32),
                pltpu.VMEM((tiles, WIDTH, 256), BF16),
                pltpu.VMEM((tiles, 1, 256), F32),
                pltpu.VMEM((tiles, WIDTH, 256), BF16),
                pltpu.VMEM((tiles, 1, 256), F32),
                pltpu.VMEM((SLOTS * WIDTH, GROUP * 256), BF16),
                pltpu.VMEM((CELLS, GROUP * 256), BF16),
                pltpu.VMEM((SLOTS * WIDTH, CELLS), F32),
                pltpu.VMEM((SLOTS * WIDTH, D), BF16),
                pltpu.VMEM((9, D, D), BF16),
                pltpu.VMEM((80, CELLS), BF16),
                pltpu.VMEM((768, 256), BF16),
                pltpu.VMEM((4, 8, 16, D), BF16),
                pltpu.VMEM((80, D), BF16),
                pltpu.VMEM((256, D), BF16),
                pltpu.VMEM((4, 12, 2, 16, D), BF16),
                pltpu.SemaphoreType.DMA((2,)),
                pltpu.SemaphoreType.DMA((2 * groups,)),
                pltpu.SemaphoreType.DMA((4,)),
                pltpu.SemaphoreType.DMA((4,)),
                pltpu.SemaphoreType.DMA((8,)),
                pltpu.SemaphoreType.DMA((9,)),
                pltpu.SemaphoreType.DMA((9,)),
            ],
            compiler_params=pltpu.CompilerParams(
                collective_id=0, has_side_effects=True, vmem_limit_bytes=60 << 20
            ),
        )(
            jnp.transpose(obs_values, (1, 0, 2)),
            obs_offset,
            obs_cell,
            obs_slot,
            obs_count,
            embed_weight,
            embed_bias[None],
            stride_weight,
            stride_bias[None],
            depth_weight,
            norm_gain[None],
            jnp.asarray(strips, BF16),
            jnp.asarray(rims, BF16),
        )

    placed = (
        P(("lon", "lat"), None, None),
        P(("lon", "lat"), None, None),
        P(("lon", "lat"), None),
        P(("lon", "lat"), None),
        P(("lon", "lat"), None),
        P(),
        P(),
        P(),
        P(),
        P(),
        P(),
    )
    return jax.shard_map(
        on_device, mesh=mesh, in_specs=placed, out_specs=P("lat", "lon", None), check_vma=False
    )
```

```python
import functools

import jax
import jax.numpy as jnp
import numpy as np
from jax import lax
from jax.experimental import pallas as pl
from jax.experimental.pallas import tpu as pltpu
from jax.sharding import PartitionSpec as P

MESH = pl.DeviceIdType.MESH
D = 256
OBS_VARS = 31
WIDTH = 32
SLOTS = 12
TLAT = 16
TLON = 32
CELLS = 512
GROUP = 8
BF16 = jnp.bfloat16
F32 = jnp.float32
PITCH = 136


def cell_number(row, col):
    return ((row % 2) * 2 + col % 2) * 128 + (row // 2) * 16 + col // 2


def strip_table():
    table = np.zeros((80, CELLS), np.float32)
    for row in range(TLAT):
        for i in range(3):
            table[row * 3 + i, cell_number(row, TLON - 3 + i)] = 1
        for i in range(2):
            table[48 + row * 2 + i, cell_number(row, i)] = 1
    return table


def rim_table():
    table = np.zeros((4, 12, 16, 256), np.float32)
    for plane in range(4):
        row_odd, col_odd = divmod(plane, 2)
        for p in range(-2, 9):
            row = 2 * p + row_odd
            if row < -3 or row > 17:
                continue
            for q in (-2, -1, 16):
                if q == -2 and not col_odd:
                    continue
                if q < 0:
                    i = 2 * q + col_odd + 3
                    if row < 0:
                        source = 80 + (row + 16) * 3 + i - 32
                    elif row < 16:
                        source = row * 3 + i
                    else:
                        source = 112 + (row - 16) * 3 + i
                    table[plane, p + 2, 16 + q, source] = 1
                else:
                    i = col_odd
                    if row < 0:
                        source = 96 + (row + 16) * 2 + i - 16
                    elif row < 16:
                        source = 48 + row * 2 + i
                    else:
                        source = 128 + (row - 16) * 2 + i
                    table[plane, p + 3, 0, source] = 1
    return table.reshape(4 * 12 * 16, 256)


def gelu(x):
    return 0.5 * x * (1.0 + jnp.tanh(0.7978845608028654 * (x + 0.044715 * (x * x * x))))


def scrambled(dims):
    nx, nz, nc, ny = dims
    offsets = [
        (dx, dz, dc, dy)
        for dx in range(nx)
        for dz in range(nz)
        for dc in range(nc)
        for dy in range(ny)
        if dx or dz or dc or dy
    ]
    return sorted(offsets, key=lambda o: (o[0] * 37 + o[1] * 59 + o[2] * 19 + o[3] * 101) % 127)


def kernel(
    dims,
    values_ref,
    offset_hbm,
    cell_hbm,
    slot_hbm,
    count_hbm,
    embed_weight_hbm,
    embed_bias_hbm,
    stride_weight_hbm,
    stride_bias_hbm,
    depth_weight_hbm,
    gain_hbm,
    strip_hbm,
    rim_hbm,
    out_ref,
    offset_ref,
    cell_ref,
    slot_ref,
    count_ref,
    embed_bias_ref,
    stride_bias_ref,
    depth_weight_ref,
    gain_ref,
    raw_ref,
    wide_ref,
    packed_ref,
    code_ref,
    recv_ref,
    recv_code_ref,
    spread_ref,
    hot_ref,
    total_ref,
    embed_weight_ref,
    stride_weight_ref,
    strip_ref,
    rim_ref,
    tile_ref,
    strips_ref,
    halo_ref,
    framed_ref,
    send_sem,
    recv_sem,
    first_sem,
    raw_sem,
    load_sem,
    halo_send_sem,
    halo_recv_sem,
):
    nx, nz, nc, ny = dims
    lons = nx * nz * nc
    tiles = lons * ny
    groups = tiles // GROUP
    lon, lat = lax.axis_index("lon"), lax.axis_index("lat")
    core = lon % nc
    z = (lon // nc) % nz
    x = lon // (nc * nz)

    def wrapped(value, size):
        return jnp.where(value >= size, value - size, value)

    at_x = [wrapped(x + i, nx) * (nz * nc) for i in range(nx)]
    at_z = [wrapped(z + i, nz) * nc for i in range(nz)]
    at_core = [wrapped(core + i, nc) for i in range(nc)]
    at_y = [wrapped(lat + i, ny) for i in range(ny)]
    order = scrambled(dims)
    partners = [(at_x[o[0]] + at_z[o[1]] + at_core[o[2]], at_y[o[3]]) for o in order]

    barrier = pltpu.get_barrier_semaphore()
    def reach(o):
        return min(o[0], nx - o[0]) + min(o[1], nz - o[1]) + min(o[3], ny - o[3])

    greeted = sorted(range(len(order)), key=lambda i: -reach(order[i]))
    for partner in [partners[i] for i in greeted]:
        pl.semaphore_signal(barrier, inc=1, device_id=partner, device_id_type=MESH)

    firsts = [
        pltpu.make_async_copy(source, target, first_sem.at[i])
        for i, (source, target) in enumerate(
            (
                (offset_hbm, offset_ref),
                (count_hbm, count_ref),
                (cell_hbm, cell_ref),
                (slot_hbm, slot_ref),
            )
        )
    ]
    for first in firsts:
        first.start()
    chunks = ((0, 8), (8, 16), (16, 24), (24, 31))
    raws = [
        pltpu.make_async_copy(
            values_ref.at[low:high], raw_ref.at[low:high], raw_sem.at[i]
        )
        for i, (low, high) in enumerate(chunks)
    ]
    for raw in raws:
        raw.start()
    halo_ref[...] = jnp.zeros_like(halo_ref)
    me = lon * ny + lat
    loads = [
        pltpu.make_async_copy(source, target, load_sem.at[i])
        for i, (source, target) in enumerate(
            (
                (embed_weight_hbm, embed_weight_ref),
                (stride_weight_hbm, stride_weight_ref),
                (strip_hbm, strip_ref),
                (rim_hbm, rim_ref),
                (embed_bias_hbm, embed_bias_ref),
                (stride_bias_hbm, stride_bias_ref),
                (depth_weight_hbm, depth_weight_ref),
                (gain_hbm, gain_ref),
            )
        )
    ]
    for first in firsts:
        first.wait()

    lane = lax.broadcasted_iota(jnp.int32, (tiles, tiles), 1)
    line = lax.broadcasted_iota(jnp.int32, (tiles, tiles), 0)
    count = jnp.sum(
        jnp.where(lane == line, count_ref[...].astype(F32), 0.0), axis=1, keepdims=True
    )
    position = lax.broadcasted_iota(jnp.int32, cell_ref.shape, 1).astype(F32)
    off_y, off_x = offset_ref[:, 0, :], offset_ref[:, 1, :]
    weight = jnp.where(position < count, jnp.exp(-2.0 * (off_y * off_y + off_x * off_x)), 0.0)
    cell = cell_ref[...]
    row, col = cell >> 5, cell & 31
    code = (
        slot_ref[...] * CELLS
        + (((row & 1) * 2 + (col & 1)) * 128 + (row >> 1) * 16 + (col >> 1))
    ).astype(F32)
    code_ref[:, 0, :] = code
    def widen(k, row):
        for h in range(2):
            start = (h * WIDTH + k) * PITCH
            wide_ref[start : start + tiles] = row[:, h * 128 : h * 128 + 128]

    widen(31, weight)
    for raw, (low, high) in zip(raws, chunks):
        raw.wait()
        for k in range(low, high):
            widen(k, raw_ref[k].astype(F32) * weight)

    def pack(target):
        halves = [
            wide_ref[pl.ds(target + h * WIDTH * PITCH, WIDTH, stride=PITCH), :] for h in range(2)
        ]
        return jnp.concatenate(halves, axis=1).astype(BF16)

    pl.semaphore_wait(barrier, tiles - 1)

    def send_values(source, target, sem, partner):
        return pltpu.make_async_remote_copy(
            packed_ref.at[source],
            recv_ref.at[target],
            send_sem.at[0],
            recv_sem.at[sem],
            device_id=partner,
            device_id_type=MESH,
        )

    def send_code(source, target, sem, partner):
        return pltpu.make_async_remote_copy(
            code_ref.at[source],
            recv_code_ref.at[target],
            send_sem.at[1],
            recv_sem.at[sem + groups],
            device_id=partner,
            device_id_type=MESH,
        )

    for i, partner in enumerate(partners, 1):
        to = partner[0] * ny + partner[1]
        packed_ref[i] = pack(to)
        send_code(to, i, i // GROUP, partner).start()
        send_values(i, i, i // GROUP, partner).start()

    for load in loads:
        load.start()
    recv_ref[0] = pack(me)
    recv_code_ref[0] = code_ref[me]
    total_ref[...] = jnp.zeros_like(total_ref)

    line16 = lax.broadcasted_iota(jnp.int32, (16, 256), 0).astype(F32).astype(BF16)

    def scatter(group):
        def build(i, carry):
            at = group * GROUP + i
            code = recv_code_ref[at]
            slot = jnp.floor(code * (1.0 / CELLS))
            cell = code - slot * CELLS
            half = jnp.where(cell >= 256, 1.0, 0.0)
            low = cell - 256.0 * half
            first = jnp.broadcast_to(jnp.where(half == 0.0, low, -1.0), (16, 256)).astype(BF16)
            second = jnp.broadcast_to(jnp.where(half == 1.0, low, -1.0), (16, 256)).astype(BF16)
            slot = jnp.broadcast_to(slot, (16, 256)).astype(BF16)
            packed = recv_ref[at]
            lanes = pl.ds(pl.multiple_of(i * 256, 256), 256)
            zero, one = jnp.zeros((16, 256), BF16), jnp.ones((16, 256), BF16)
            for s in range(SLOTS):
                mine = slot == s
                for h in range(2):
                    spread_ref[s * WIDTH + h * 16 : s * WIDTH + h * 16 + 16, lanes] = jnp.where(
                        mine, packed[h * 16 : h * 16 + 16], zero
                    )
            for h, wanted in enumerate((first, second)):
                for r in range(16):
                    at_row = h * 256 + r * 16
                    hot_ref[at_row : at_row + 16, lanes] = jnp.where(
                        wanted == line16 + (r * 16), one, zero
                    )
            return carry

        lax.fori_loop(0, GROUP, build, 0, unroll=True)
        total_ref[...] += lax.dot_general(
            spread_ref[...],
            hot_ref[...],
            (((1,), (1,)), ((), ())),
            preferred_element_type=F32,
        )

    def arrive(group, first, size):
        send_code(pl.ds(first, size), pl.ds(first, size), group, partners[0]).wait_recv()
        send_values(pl.ds(first, size), pl.ds(first, size), group, partners[0]).wait_recv()

    def group_step(group, carry):
        @pl.when(group == 0)
        def _():
            arrive(0, 1, GROUP - 1)

        @pl.when(group > 0)
        def _():
            arrive(group, group * GROUP, GROUP)

        scatter(group)
        return carry

    lax.fori_loop(0, groups, group_step, 0)

    for load in loads:
        load.wait()

    total = total_ref[...].reshape(SLOTS, WIDTH, CELLS)
    density = total[:, WIDTH - 1 :, :]
    variable = lax.broadcasted_iota(jnp.int32, (SLOTS, WIDTH, CELLS), 1)
    gridded = jnp.where(variable == WIDTH - 1, total, total / (1.0 + density))
    gridded = gridded.reshape(SLOTS * WIDTH, CELLS).astype(BF16)
    projected = lax.dot_general(
        gridded, embed_weight_ref[...], (((0,), (0,)), ((), ())), preferred_element_type=F32
    )
    embedded = gelu(projected + embed_bias_ref[...]).astype(BF16)
    tile_ref[...] = embedded.reshape(4, 8, 16, D)

    right, left = wrapped(lon + 1, lons), wrapped(lon + lons - 1, lons)
    below, above = wrapped(lat + 1, ny), wrapped(lat + ny - 1, ny)

    def rows(i, source, target, partner):
        return pltpu.make_async_remote_copy(
            source,
            target,
            halo_send_sem.at[i],
            halo_recv_sem.at[i],
            device_id=partner,
            device_id_type=MESH,
        )

    exchange = [
        rows(0, tile_ref.at[2:4, 6:8], framed_ref.at[2:4, 0:2, 1], (lon, below)),
        rows(1, tile_ref.at[0:2, 7:8], framed_ref.at[0:2, 1:2, 1], (lon, below)),
        rows(2, tile_ref.at[0:4, 0:1], framed_ref.at[0:4, 10:11, 1], (lon, above)),
        rows(3, strips_ref.at[0:48], halo_ref.at[0:48], (right, lat)),
        rows(4, strips_ref.at[48:80], halo_ref.at[48:80], (left, lat)),
        rows(5, strips_ref.at[32:48], halo_ref.at[80:96], (right, below)),
        rows(6, strips_ref.at[64:80], halo_ref.at[96:112], (left, below)),
        rows(7, strips_ref.at[0:16], halo_ref.at[112:128], (right, above)),
        rows(8, strips_ref.at[48:64], halo_ref.at[128:144], (left, above)),
    ]
    for copy in exchange[:3]:
        copy.start()
    strips_ref[...] = jnp.dot(strip_ref[...], embedded, preferred_element_type=F32).astype(BF16)
    for copy in exchange[3:]:
        copy.start()
    framed_ref[:, 2:10, 1] = embedded.reshape(4, 8, 16, D)
    for copy in exchange:
        copy.wait_recv()

    @pl.when(lat == 0)
    def _():
        halo_ref[80:112] = jnp.zeros((32, D), BF16)
        framed_ref[2:4, 1, 1] = jnp.zeros((2, 16, D), BF16)

    rim = jnp.dot(rim_ref[...], halo_ref[...], preferred_element_type=F32).astype(BF16)
    framed_ref[:, :, 0] = rim.reshape(4, 12, 16, D)

    planes = [framed_ref[i].reshape(384, D) for i in range(4)]
    span = 336

    def tap(a, c):
        plane = planes[(0 if a == 1 else 2) + (0 if c == 1 else 1)]
        base = 0 if a == 0 else 32
        return jnp.dot(
            plane[base : base + span], stride_weight_ref[3 * a + c], preferred_element_type=F32
        )

    before = tap(0, 0) + tap(1, 0) + tap(2, 0)
    here = tap(0, 1) + tap(1, 1) + tap(2, 1) + tap(0, 2) + tap(1, 2) + tap(2, 2)
    strided = pltpu.roll(before, 1, 0) + here + stride_bias_ref[...]
    coarse = gelu(strided).astype(BF16).astype(F32)
    at = lax.broadcasted_iota(jnp.int32, (span, D), 0)
    low = jnp.where(lat == 0, 40, 0)
    high = jnp.where(lat == ny - 1, 296, span)
    coarse = jnp.where((at >= low) & (at < high), coarse, 0.0)

    reach = 272

    def column(c):
        total = coarse[0:reach] * depth_weight_ref[c : c + 1]
        for a in (1, 2):
            total = total + coarse[32 * a : 32 * a + reach] * depth_weight_ref[3 * a + c : 3 * a + c + 1]
        return total

    mixed = (
        coarse[32 : 32 + reach]
        + column(1)
        + pltpu.roll(column(0), 1, 0)
        + pltpu.roll(column(2), reach - 1, 0)
    )
    mixed = mixed[:256].reshape(8, 2, 16, D)[:, 1]
    centre = mixed - jnp.mean(mixed, axis=-1, keepdims=True)
    variance = jnp.mean(centre * centre, axis=-1, keepdims=True)
    out_ref[...] = (centre * lax.rsqrt(variance + 1e-05) * gain_ref[...][None]).astype(BF16)

    for copy in exchange:
        copy.wait_send()
    send_code(pl.ds(1, tiles - 1), pl.ds(1, tiles - 1), 0, partners[0]).wait_send()
    send_values(pl.ds(1, tiles - 1), pl.ds(1, tiles - 1), 0, partners[0]).wait_send()


def physical(lons, lats):
    nc = 2
    nz = 4 if lons % 8 == 0 else 2
    return (lons // (nc * nz), nz, nc, lats)


def solution(mesh):
    dims = physical(mesh.shape["lon"], mesh.shape["lat"])
    tiles = mesh.shape["lon"] * mesh.shape["lat"]
    groups = tiles // GROUP
    vmem = pl.BlockSpec(memory_space=pltpu.VMEM)
    anywhere = pl.BlockSpec(memory_space=pl.ANY)
    strips, rims = strip_table(), rim_table()

    def on_device(
        obs_values,
        obs_offset,
        obs_cell,
        obs_slot,
        obs_count,
        embed_weight,
        embed_bias,
        stride_weight,
        stride_bias,
        depth_weight,
        norm_gain,
    ):
        return pl.pallas_call(
            functools.partial(kernel, dims),
            out_shape=pltpu.VMEM((TLAT // 2, TLON // 2, D), BF16),
            in_specs=[anywhere] * 13,
            out_specs=vmem,
            scratch_shapes=[
                pltpu.VMEM((tiles, 2, 256), F32),
                pltpu.VMEM((tiles, 256), jnp.int32),
                pltpu.VMEM((tiles, 256), jnp.int32),
                pltpu.VMEM((1, tiles), jnp.int32),
                pltpu.VMEM((1, D), F32),
                pltpu.VMEM((1, D), F32),
                pltpu.VMEM((9, D), F32),
                pltpu.VMEM((1, D), F32),
                pltpu.VMEM((OBS_VARS, tiles, 256), BF16),
                pltpu.VMEM((2 * WIDTH * PITCH, 128), F32),
                pltpu.VMEM((tiles, WIDTH, 256), BF16),
                pltpu.VMEM((tiles, 1, 256), F32),
                pltpu.VMEM((tiles, WIDTH, 256), BF16),
                pltpu.VMEM((tiles, 1, 256), F32),
                pltpu.VMEM((SLOTS * WIDTH, GROUP * 256), BF16),
                pltpu.VMEM((CELLS, GROUP * 256), BF16),
                pltpu.VMEM((SLOTS * WIDTH, CELLS), F32),
                pltpu.VMEM((SLOTS * WIDTH, D), BF16),
                pltpu.VMEM((9, D, D), BF16),
                pltpu.VMEM((80, CELLS), BF16),
                pltpu.VMEM((768, 256), BF16),
                pltpu.VMEM((4, 8, 16, D), BF16),
                pltpu.VMEM((80, D), BF16),
                pltpu.VMEM((256, D), BF16),
                pltpu.VMEM((4, 12, 2, 16, D), BF16),
                pltpu.SemaphoreType.DMA((2,)),
                pltpu.SemaphoreType.DMA((2 * groups,)),
                pltpu.SemaphoreType.DMA((4,)),
                pltpu.SemaphoreType.DMA((4,)),
                pltpu.SemaphoreType.DMA((8,)),
                pltpu.SemaphoreType.DMA((9,)),
                pltpu.SemaphoreType.DMA((9,)),
            ],
            compiler_params=pltpu.CompilerParams(
                collective_id=0, has_side_effects=True, vmem_limit_bytes=60 << 20
            ),
        )(
            jnp.transpose(obs_values, (1, 0, 2)),
            obs_offset,
            obs_cell,
            obs_slot,
            obs_count,
            embed_weight,
            embed_bias[None],
            stride_weight,
            stride_bias[None],
            depth_weight,
            norm_gain[None],
            jnp.asarray(strips, BF16),
            jnp.asarray(rims, BF16),
        )

    placed = (
        P(("lon", "lat"), None, None),
        P(("lon", "lat"), None, None),
        P(("lon", "lat"), None),
        P(("lon", "lat"), None),
        P(("lon", "lat"), None),
        P(),
        P(),
        P(),
        P(),
        P(),
        P(),
    )
    return jax.shard_map(
        on_device, mesh=mesh, in_specs=placed, out_specs=P("lat", "lon", None), check_vma=False
    )
```

```python
import functools

import jax
import jax.numpy as jnp
import numpy as np
from jax import lax
from jax.experimental import pallas as pl
from jax.experimental.pallas import tpu as pltpu
from jax.sharding import PartitionSpec as P

MESH = pl.DeviceIdType.MESH
D = 256
OBS_VARS = 31
WIDTH = 32
SLOTS = 12
TLAT = 16
TLON = 32
CELLS = 512
GROUP = 8
BF16 = jnp.bfloat16
F32 = jnp.float32
PITCH = 136


def cell_number(row, col):
    return ((row % 2) * 2 + col % 2) * 128 + (row // 2) * 16 + col // 2


def strip_table():
    table = np.zeros((80, CELLS), np.float32)
    for row in range(TLAT):
        for i in range(3):
            table[row * 3 + i, cell_number(row, TLON - 3 + i)] = 1
        for i in range(2):
            table[48 + row * 2 + i, cell_number(row, i)] = 1
    return table


def rim_table():
    table = np.zeros((4, 12, 16, 256), np.float32)
    for plane in range(4):
        row_odd, col_odd = divmod(plane, 2)
        for p in range(-2, 9):
            row = 2 * p + row_odd
            if row < -3 or row > 17:
                continue
            for q in (-2, -1, 16):
                if q == -2 and not col_odd:
                    continue
                if q < 0:
                    i = 2 * q + col_odd + 3
                    if row < 0:
                        source = 80 + (row + 16) * 3 + i - 32
                    elif row < 16:
                        source = row * 3 + i
                    else:
                        source = 112 + (row - 16) * 3 + i
                    table[plane, p + 2, 16 + q, source] = 1
                else:
                    i = col_odd
                    if row < 0:
                        source = 96 + (row + 16) * 2 + i - 16
                    elif row < 16:
                        source = 48 + row * 2 + i
                    else:
                        source = 128 + (row - 16) * 2 + i
                    table[plane, p + 3, 0, source] = 1
    return table.reshape(4 * 12 * 16, 256)


def gelu(x):
    return 0.5 * x * (1.0 + jnp.tanh(0.7978845608028654 * (x + 0.044715 * (x * x * x))))


def scrambled(dims):
    nx, nz, nc, ny = dims
    offsets = [
        (dx, dz, dc, dy)
        for dx in range(nx)
        for dz in range(nz)
        for dc in range(nc)
        for dy in range(ny)
        if dx or dz or dc or dy
    ]
    return sorted(offsets, key=lambda o: (o[0] * 37 + o[1] * 59 + o[2] * 83 + o[3] * 101) % 127)


def kernel(
    dims,
    values_ref,
    offset_hbm,
    cell_hbm,
    slot_hbm,
    count_hbm,
    embed_weight_hbm,
    embed_bias_hbm,
    stride_weight_hbm,
    stride_bias_hbm,
    depth_weight_hbm,
    gain_hbm,
    strip_hbm,
    rim_hbm,
    out_ref,
    offset_ref,
    cell_ref,
    slot_ref,
    count_ref,
    embed_bias_ref,
    stride_bias_ref,
    depth_weight_ref,
    gain_ref,
    raw_ref,
    wide_ref,
    packed_ref,
    code_ref,
    recv_ref,
    recv_code_ref,
    spread_ref,
    hot_ref,
    total_ref,
    embed_weight_ref,
    stride_weight_ref,
    strip_ref,
    rim_ref,
    tile_ref,
    strips_ref,
    halo_ref,
    framed_ref,
    send_sem,
    recv_sem,
    first_sem,
    raw_sem,
    load_sem,
    halo_send_sem,
    halo_recv_sem,
):
    nx, nz, nc, ny = dims
    lons = nx * nz * nc
    tiles = lons * ny
    groups = tiles // GROUP
    lon, lat = lax.axis_index("lon"), lax.axis_index("lat")
    core = lon % nc
    z = (lon // nc) % nz
    x = lon // (nc * nz)

    def wrapped(value, size):
        return jnp.where(value >= size, value - size, value)

    at_x = [wrapped(x + i, nx) * (nz * nc) for i in range(nx)]
    at_z = [wrapped(z + i, nz) * nc for i in range(nz)]
    at_core = [wrapped(core + i, nc) for i in range(nc)]
    at_y = [wrapped(lat + i, ny) for i in range(ny)]
    order = scrambled(dims)
    partners = [(at_x[o[0]] + at_z[o[1]] + at_core[o[2]], at_y[o[3]]) for o in order]

    barrier = pltpu.get_barrier_semaphore()
    def reach(o):
        return min(o[0], nx - o[0]) + min(o[1], nz - o[1]) + min(o[3], ny - o[3])

    greeted = sorted(range(len(order)), key=lambda i: -reach(order[i]))
    for partner in [partners[i] for i in greeted]:
        pl.semaphore_signal(barrier, inc=1, device_id=partner, device_id_type=MESH)

    firsts = [
        pltpu.make_async_copy(source, target, first_sem.at[i])
        for i, (source, target) in enumerate(
            (
                (offset_hbm, offset_ref),
                (count_hbm, count_ref),
                (cell_hbm, cell_ref),
                (slot_hbm, slot_ref),
            )
        )
    ]
    for first in firsts:
        first.start()
    chunks = ((0, 8), (8, 16), (16, 24), (24, 31))
    raws = [
        pltpu.make_async_copy(
            values_ref.at[low:high], raw_ref.at[low:high], raw_sem.at[i]
        )
        for i, (low, high) in enumerate(chunks)
    ]
    for raw in raws:
        raw.start()
    halo_ref[...] = jnp.zeros_like(halo_ref)
    me = lon * ny + lat
    loads = [
        pltpu.make_async_copy(source, target, load_sem.at[i])
        for i, (source, target) in enumerate(
            (
                (embed_weight_hbm, embed_weight_ref),
                (stride_weight_hbm, stride_weight_ref),
                (strip_hbm, strip_ref),
                (rim_hbm, rim_ref),
                (embed_bias_hbm, embed_bias_ref),
                (stride_bias_hbm, stride_bias_ref),
                (depth_weight_hbm, depth_weight_ref),
                (gain_hbm, gain_ref),
            )
        )
    ]
    for first in firsts:
        first.wait()

    lane = lax.broadcasted_iota(jnp.int32, (tiles, tiles), 1)
    line = lax.broadcasted_iota(jnp.int32, (tiles, tiles), 0)
    count = jnp.sum(
        jnp.where(lane == line, count_ref[...].astype(F32), 0.0), axis=1, keepdims=True
    )
    position = lax.broadcasted_iota(jnp.int32, cell_ref.shape, 1).astype(F32)
    off_y, off_x = offset_ref[:, 0, :], offset_ref[:, 1, :]
    weight = jnp.where(position < count, jnp.exp(-2.0 * (off_y * off_y + off_x * off_x)), 0.0)
    cell = cell_ref[...]
    row, col = cell >> 5, cell & 31
    code = (
        slot_ref[...] * CELLS
        + (((row & 1) * 2 + (col & 1)) * 128 + (row >> 1) * 16 + (col >> 1))
    ).astype(F32)
    code_ref[:, 0, :] = code
    def widen(k, row):
        for h in range(2):
            start = (h * WIDTH + k) * PITCH
            wide_ref[start : start + tiles] = row[:, h * 128 : h * 128 + 128]

    widen(31, weight)
    for raw, (low, high) in zip(raws, chunks):
        raw.wait()
        for k in range(low, high):
            widen(k, raw_ref[k].astype(F32) * weight)

    def pack(target):
        halves = [
            wide_ref[pl.ds(target + h * WIDTH * PITCH, WIDTH, stride=PITCH), :] for h in range(2)
        ]
        return jnp.concatenate(halves, axis=1).astype(BF16)

    pl.semaphore_wait(barrier, tiles - 1)

    def send_values(source, target, sem, partner):
        return pltpu.make_async_remote_copy(
            packed_ref.at[source],
            recv_ref.at[target],
            send_sem.at[0],
            recv_sem.at[sem],
            device_id=partner,
            device_id_type=MESH,
        )

    def send_code(source, target, sem, partner):
        return pltpu.make_async_remote_copy(
            code_ref.at[source],
            recv_code_ref.at[target],
            send_sem.at[1],
            recv_sem.at[sem + groups],
            device_id=partner,
            device_id_type=MESH,
        )

    for i, partner in enumerate(partners, 1):
        to = partner[0] * ny + partner[1]
        packed_ref[i] = pack(to)
        send_code(to, i, i // GROUP, partner).start()
        send_values(i, i, i // GROUP, partner).start()

    for load in loads:
        load.start()
    recv_ref[0] = pack(me)
    recv_code_ref[0] = code_ref[me]
    total_ref[...] = jnp.zeros_like(total_ref)

    line16 = lax.broadcasted_iota(jnp.int32, (16, 256), 0).astype(F32).astype(BF16)

    def scatter(group):
        def build(i, carry):
            at = group * GROUP + i
            code = recv_code_ref[at]
            slot = jnp.floor(code * (1.0 / CELLS))
            cell = code - slot * CELLS
            half = jnp.where(cell >= 256, 1.0, 0.0)
            low = cell - 256.0 * half
            first = jnp.broadcast_to(jnp.where(half == 0.0, low, -1.0), (16, 256)).astype(BF16)
            second = jnp.broadcast_to(jnp.where(half == 1.0, low, -1.0), (16, 256)).astype(BF16)
            slot = jnp.broadcast_to(slot, (16, 256)).astype(BF16)
            packed = recv_ref[at]
            lanes = pl.ds(pl.multiple_of(i * 256, 256), 256)
            zero, one = jnp.zeros((16, 256), BF16), jnp.ones((16, 256), BF16)
            for s in range(SLOTS):
                mine = slot == s
                for h in range(2):
                    spread_ref[s * WIDTH + h * 16 : s * WIDTH + h * 16 + 16, lanes] = jnp.where(
                        mine, packed[h * 16 : h * 16 + 16], zero
                    )
            for h, wanted in enumerate((first, second)):
                for r in range(16):
                    at_row = h * 256 + r * 16
                    hot_ref[at_row : at_row + 16, lanes] = jnp.where(
                        wanted == line16 + (r * 16), one, zero
                    )
            return carry

        lax.fori_loop(0, GROUP, build, 0, unroll=True)
        total_ref[...] += lax.dot_general(
            spread_ref[...],
            hot_ref[...],
            (((1,), (1,)), ((), ())),
            preferred_element_type=F32,
        )

    def arrive(group, first, size):
        send_code(pl.ds(first, size), pl.ds(first, size), group, partners[0]).wait_recv()
        send_values(pl.ds(first, size), pl.ds(first, size), group, partners[0]).wait_recv()

    def group_step(group, carry):
        @pl.when(group == 0)
        def _():
            arrive(0, 1, GROUP - 1)

        @pl.when(group > 0)
        def _():
            arrive(group, group * GROUP, GROUP)

        scatter(group)
        return carry

    lax.fori_loop(0, groups, group_step, 0)

    for load in loads:
        load.wait()

    total = total_ref[...].reshape(SLOTS, WIDTH, CELLS)
    density = total[:, WIDTH - 1 :, :]
    variable = lax.broadcasted_iota(jnp.int32, (SLOTS, WIDTH, CELLS), 1)
    gridded = jnp.where(variable == WIDTH - 1, total, total / (1.0 + density))
    gridded = gridded.reshape(SLOTS * WIDTH, CELLS).astype(BF16)
    projected = lax.dot_general(
        gridded, embed_weight_ref[...], (((0,), (0,)), ((), ())), preferred_element_type=F32
    )
    embedded = gelu(projected + embed_bias_ref[...]).astype(BF16)
    tile_ref[...] = embedded.reshape(4, 8, 16, D)

    right, left = wrapped(lon + 1, lons), wrapped(lon + lons - 1, lons)
    below, above = wrapped(lat + 1, ny), wrapped(lat + ny - 1, ny)

    def rows(i, source, target, partner):
        return pltpu.make_async_remote_copy(
            source,
            target,
            halo_send_sem.at[i],
            halo_recv_sem.at[i],
            device_id=partner,
            device_id_type=MESH,
        )

    exchange = [
        rows(0, tile_ref.at[2:4, 6:8], framed_ref.at[2:4, 0:2, 1], (lon, below)),
        rows(1, tile_ref.at[0:2, 7:8], framed_ref.at[0:2, 1:2, 1], (lon, below)),
        rows(2, tile_ref.at[0:4, 0:1], framed_ref.at[0:4, 10:11, 1], (lon, above)),
        rows(3, strips_ref.at[0:48], halo_ref.at[0:48], (right, lat)),
        rows(4, strips_ref.at[48:80], halo_ref.at[48:80], (left, lat)),
        rows(5, strips_ref.at[32:48], halo_ref.at[80:96], (right, below)),
        rows(6, strips_ref.at[64:80], halo_ref.at[96:112], (left, below)),
        rows(7, strips_ref.at[0:16], halo_ref.at[112:128], (right, above)),
        rows(8, strips_ref.at[48:64], halo_ref.at[128:144], (left, above)),
    ]
    for copy in exchange[:3]:
        copy.start()
    strips_ref[...] = jnp.dot(strip_ref[...], embedded, preferred_element_type=F32).astype(BF16)
    for copy in exchange[3:]:
        copy.start()
    framed_ref[:, 2:10, 1] = embedded.reshape(4, 8, 16, D)
    send_code(pl.ds(1, tiles - 1), pl.ds(1, tiles - 1), 0, partners[0]).wait_send()
    send_values(pl.ds(1, tiles - 1), pl.ds(1, tiles - 1), 0, partners[0]).wait_send()
    for copy in exchange:
        copy.wait_recv()

    @pl.when(lat == 0)
    def _():
        halo_ref[80:112] = jnp.zeros((32, D), BF16)
        framed_ref[2:4, 1, 1] = jnp.zeros((2, 16, D), BF16)

    rim = jnp.dot(rim_ref[...], halo_ref[...], preferred_element_type=F32).astype(BF16)
    framed_ref[:, :, 0] = rim.reshape(4, 12, 16, D)

    planes = [framed_ref[i].reshape(384, D) for i in range(4)]
    span = 336

    def tap(a, c):
        plane = planes[(0 if a == 1 else 2) + (0 if c == 1 else 1)]
        base = 0 if a == 0 else 32
        return jnp.dot(
            plane[base : base + span], stride_weight_ref[3 * a + c], preferred_element_type=F32
        )

    before = tap(0, 0) + tap(1, 0) + tap(2, 0)
    here = tap(0, 1) + tap(1, 1) + tap(2, 1) + tap(0, 2) + tap(1, 2) + tap(2, 2)
    strided = pltpu.roll(before, 1, 0) + here + stride_bias_ref[...]
    coarse = gelu(strided).astype(BF16).astype(F32)
    at = lax.broadcasted_iota(jnp.int32, (span, D), 0)
    low = jnp.where(lat == 0, 40, 0)
    high = jnp.where(lat == ny - 1, 296, span)
    coarse = jnp.where((at >= low) & (at < high), coarse, 0.0)

    reach = 272

    def column(c):
        total = coarse[0:reach] * depth_weight_ref[c : c + 1]
        for a in (1, 2):
            total = total + coarse[32 * a : 32 * a + reach] * depth_weight_ref[3 * a + c : 3 * a + c + 1]
        return total

    mixed = (
        coarse[32 : 32 + reach]
        + column(1)
        + pltpu.roll(column(0), 1, 0)
        + pltpu.roll(column(2), reach - 1, 0)
    )
    mixed = mixed[:256].reshape(8, 2, 16, D)[:, 1]
    centre = mixed - jnp.mean(mixed, axis=-1, keepdims=True)
    variance = jnp.mean(centre * centre, axis=-1, keepdims=True)
    out_ref[...] = (centre * lax.rsqrt(variance + 1e-05) * gain_ref[...][None]).astype(BF16)

    for copy in exchange:
        copy.wait_send()


def physical(lons, lats):
    nc = 2
    nz = 4 if lons % 8 == 0 else 2
    return (lons // (nc * nz), nz, nc, lats)


def solution(mesh):
    dims = physical(mesh.shape["lon"], mesh.shape["lat"])
    tiles = mesh.shape["lon"] * mesh.shape["lat"]
    groups = tiles // GROUP
    vmem = pl.BlockSpec(memory_space=pltpu.VMEM)
    anywhere = pl.BlockSpec(memory_space=pl.ANY)
    strips, rims = strip_table(), rim_table()

    def on_device(
        obs_values,
        obs_offset,
        obs_cell,
        obs_slot,
        obs_count,
        embed_weight,
        embed_bias,
        stride_weight,
        stride_bias,
        depth_weight,
        norm_gain,
    ):
        return pl.pallas_call(
            functools.partial(kernel, dims),
            out_shape=pltpu.VMEM((TLAT // 2, TLON // 2, D), BF16),
            in_specs=[anywhere] * 13,
            out_specs=vmem,
            scratch_shapes=[
                pltpu.VMEM((tiles, 2, 256), F32),
                pltpu.VMEM((tiles, 256), jnp.int32),
                pltpu.VMEM((tiles, 256), jnp.int32),
                pltpu.VMEM((1, tiles), jnp.int32),
                pltpu.VMEM((1, D), F32),
                pltpu.VMEM((1, D), F32),
                pltpu.VMEM((9, D), F32),
                pltpu.VMEM((1, D), F32),
                pltpu.VMEM((OBS_VARS, tiles, 256), BF16),
                pltpu.VMEM((2 * WIDTH * PITCH, 128), F32),
                pltpu.VMEM((tiles, WIDTH, 256), BF16),
                pltpu.VMEM((tiles, 1, 256), F32),
                pltpu.VMEM((tiles, WIDTH, 256), BF16),
                pltpu.VMEM((tiles, 1, 256), F32),
                pltpu.VMEM((SLOTS * WIDTH, GROUP * 256), BF16),
                pltpu.VMEM((CELLS, GROUP * 256), BF16),
                pltpu.VMEM((SLOTS * WIDTH, CELLS), F32),
                pltpu.VMEM((SLOTS * WIDTH, D), BF16),
                pltpu.VMEM((9, D, D), BF16),
                pltpu.VMEM((80, CELLS), BF16),
                pltpu.VMEM((768, 256), BF16),
                pltpu.VMEM((4, 8, 16, D), BF16),
                pltpu.VMEM((80, D), BF16),
                pltpu.VMEM((256, D), BF16),
                pltpu.VMEM((4, 12, 2, 16, D), BF16),
                pltpu.SemaphoreType.DMA((2,)),
                pltpu.SemaphoreType.DMA((2 * groups,)),
                pltpu.SemaphoreType.DMA((4,)),
                pltpu.SemaphoreType.DMA((4,)),
                pltpu.SemaphoreType.DMA((8,)),
                pltpu.SemaphoreType.DMA((9,)),
                pltpu.SemaphoreType.DMA((9,)),
            ],
            compiler_params=pltpu.CompilerParams(
                collective_id=0, has_side_effects=True, vmem_limit_bytes=60 << 20
            ),
        )(
            jnp.transpose(obs_values, (1, 0, 2)),
            obs_offset,
            obs_cell,
            obs_slot,
            obs_count,
            embed_weight,
            embed_bias[None],
            stride_weight,
            stride_bias[None],
            depth_weight,
            norm_gain[None],
            jnp.asarray(strips, BF16),
            jnp.asarray(rims, BF16),
        )

    placed = (
        P(("lon", "lat"), None, None),
        P(("lon", "lat"), None, None),
        P(("lon", "lat"), None),
        P(("lon", "lat"), None),
        P(("lon", "lat"), None),
        P(),
        P(),
        P(),
        P(),
        P(),
        P(),
    )
    return jax.shard_map(
        on_device, mesh=mesh, in_specs=placed, out_specs=P("lat", "lon", None), check_vma=False
    )
```
